512 devices in a mesh: outer: 16 (over y_hi, x), inner: 32 (over z, y_lo, core).
Axes of the slice: x: 4, y: 8 (y_hi: 4, y_lo: 2; y = y_hi * 2 + y_lo), z: 8, core: 2. Of those that a mesh axis runs over, the one named last changes fastest.
Arguments:
- queries: bfloat16 [16384, 768], P('inner'), may hold values from -8 to 8
- passages: bfloat16 [32768, 768], P(('outer', 'inner')), may hold values from -8 to 8
- positive: int32 [16384], P('inner'), may hold values from 0 to 32767
Outputs:
- query_grad: bfloat16 [16384, 768], P('inner', 'outer')
- loss: float32 [16384], P('inner')
The draws below stay inside these ranges and needn't reach their ends.
All inputs are finite; a program needn't handle non-finite values.
Results may differ from the reference program's by a relative error of at most 0.0085.
Values may be sent and summed in bfloat16 or wider, within the bound.
No kernel may reach another device: no remote copies, remote signals or barrier semaphores. Data moves between devices by JAX's collectives and lax.ppermute only.
A program may use at most 64 MiB of HBM per device.

```python
import math
import jax
import jax.numpy as jnp
from jax import lax

D = 768
Q_DEV = 512
NQ = 16384
GROUP = 2048
NPASS = 32768
N_OUTER = 16
N_INNER = 32


def aligned_rows(key):
    inner_key = jax.random.fold_in(key, 7)
    query_rows = jax.random.permutation(jax.random.fold_in(inner_key, 1), NQ)[:6]
    passage_rows = jax.random.permutation(jax.random.fold_in(inner_key, 2), NPASS)[:12]
    magnitude = jax.random.uniform(jax.random.fold_in(inner_key, 3), (6, D), jnp.float32, 0.8, 1.0)
    signs = jnp.where(jax.random.bernoulli(jax.random.fold_in(inner_key, 4), 0.5, (6, D)), 1.0, -1.0)
    first = magnitude * signs
    other = jax.random.uniform(jax.random.fold_in(inner_key, 5), (6, D), jnp.float32, -1.0, 1.0)
    other = other - (jnp.sum(other * first, 1) / jnp.sum(first * first, 1))[:, None] * first
    target = jnp.array([110.0, 160.0, 220.0, 110.0, 160.0, 220.0], jnp.float32)
    factor = jnp.sqrt(target / (3.0 / math.sqrt(D) * jnp.sum(first * first, 1)))
    lead = factor[:, None] * first
    shrink = 2.0 / target
    second = factor[:, None] * ((1.0 - shrink)[:, None] * first + 0.5 * other)
    return (query_rows, passage_rows, lead, second)


def draw_queries(key, part):
    values = jnp.clip(jax.random.normal(jax.random.fold_in(key, 11), (NQ, D), jnp.float32), -8.0, 8.0)
    query_rows, passage_rows, lead, second = aligned_rows(key)
    values = values.at[query_rows].set(lead)
    return values.astype(jnp.bfloat16)


def draw_passages(key, part):
    values = jnp.clip(jax.random.normal(jax.random.fold_in(key, 22), (NPASS, D), jnp.float32), -4.0, 4.0)
    query_rows, passage_rows, lead, second = aligned_rows(key)
    values = values.at[passage_rows[:6]].set(lead)
    values = values.at[passage_rows[6:]].set(jnp.clip(second, -8.0, 8.0))
    return values.astype(jnp.bfloat16)


def plant(drawn, stream_key, smallest, top_value):
    index_at = [jax.random.randint(jax.random.fold_in(stream_key, axis), (), 0, length) for axis, length in enumerate(drawn.shape)]
    widest = drawn.shape.index(max(drawn.shape))
    neighbour = index_at[:widest] + [(index_at[widest] + 1) % drawn.shape[widest]] + index_at[widest + 1:]
    return drawn.at[tuple(index_at)].set(smallest).at[tuple(neighbour)].set(top_value)


def setup_inputs(seed: int = 0) -> dict:
    streams_of = jax.random.split(jax.random.key(seed), 4)
    queries = draw_queries(jax.random.fold_in(streams_of[3], 71), 0)
    passages = draw_passages(jax.random.fold_in(streams_of[3], 71), 0)
    positive = plant(jax.random.randint(streams_of[2], (NQ,), 0, NPASS), jax.random.fold_in(streams_of[2], 1), 0, NPASS - 1).astype(jnp.int32)
    return dict(queries=queries, passages=passages, positive=positive)


def reference(queries, passages, positive):
    scale = 3.0 / math.sqrt(D)
    query_blocks = queries.reshape(N_INNER, Q_DEV, D)
    index_blocks = positive.reshape(N_INNER, Q_DEV)
    grouped = passages.reshape(N_OUTER, GROUP, D).astype(jnp.float32)

    def one_block(pair):
        block, picks = pair
        scores = jnp.dot(block, passages.T, preferred_element_type=jnp.float32) * scale
        top = lax.optimization_barrier(jnp.max(scores, axis=1))
        expd = jnp.exp(scores - top[:, None])
        total = lax.optimization_barrier(jnp.sum(expd, axis=1))
        weights = expd.astype(jnp.bfloat16).astype(jnp.float32).reshape(Q_DEV, N_OUTER, GROUP)
        parts = jnp.einsum('qgp,gpd->gqd', weights, grouped)
        parts = parts.astype(jnp.bfloat16).astype(jnp.float32)
        mixture = lax.optimization_barrier(jnp.sum(parts, axis=0))
        chosen = jnp.take(passages, picks.astype(jnp.int32), axis=0).astype(jnp.float32)
        pscore = jnp.take_along_axis(scores, picks.astype(jnp.int32)[:, None], axis=1)[:, 0]
        grad = (scale * (mixture / total[:, None] - chosen)).astype(jnp.bfloat16)
        loss = top + jnp.log(total) - pscore
        return (grad, loss)
    grads, losses = lax.map(one_block, (query_blocks, index_blocks))
    return (grads.reshape(NQ, D), losses.reshape(NQ))
```

```python
import math

import jax
import jax.numpy as jnp
from jax import lax
from jax.sharding import Mesh
from jax.sharding import PartitionSpec as P

INNER = ("z", "yl", "c")
OUTER = ("yh", "x")
LANE = ("yh", "yl", "c")


def swapped(x):
    return lax.ppermute(x, "c", [(0, 1), (1, 0)])


def to_sides(x, ny):
    perm = []
    for y in range(ny):
        perm.append((2 * y, 2 * ((y - 1) % ny)))
        perm.append((2 * y + 1, 2 * ((y + 1) % ny) + 1))
    return lax.ppermute(x, LANE, perm)


def dot(a, b, dims):
    return lax.dot_general(a, b, (dims, ((), ())), preferred_element_type=jnp.float32)


def part(p, q, ids, positive, scale):
    scores = dot(p, q, ((1,), (1,))) * scale
    hits = ids[:, None] == positive[None, :]
    top = jnp.max(scores, axis=0)
    expd = jnp.exp(scores - top[None, :])
    total = jnp.sum(expd, axis=0)
    pscore = jnp.sum(jnp.where(hits, scores, 0.0), axis=0)
    mix = dot(p, expd.astype(jnp.bfloat16), ((0,), (0,)))
    chosen = dot(p, hits.astype(jnp.bfloat16), ((0,), (0,)))
    return top, total, pscore, mix, chosen


def shards(queries, passages, positive):
    count, width = queries.shape
    rows = passages.shape[0]
    scale = 3.0 / math.sqrt(width)
    nz, nx = lax.axis_size("z"), lax.axis_size("x")
    ny = lax.axis_size("yh") * 2
    x, c = lax.axis_index("x"), lax.axis_index("c")
    y = lax.axis_index("yh") * 2 + lax.axis_index("yl")

    def ids_of(yy, cc):
        yy = yy % ny
        first = (((yy // 2) * nx + x) * nz * 2 + yy % 2) * 2 + cc
        local = lax.broadcasted_iota(jnp.int32, (nz, rows), 1)
        z = lax.broadcasted_iota(jnp.int32, (nz, rows), 0)
        return ((first + z * 4) * rows + local).reshape(-1)

    copies = jnp.broadcast_to(passages, (nz, rows, width))
    column = lax.all_to_all(copies, "z", split_axis=0, concat_axis=0, tiled=True)
    column = column.reshape(nz * rows, width)
    side = to_sides(column, ny)
    column2 = swapped(column)
    side2 = swapped(side)

    own = jnp.concatenate([column, column2], axis=0)
    own_ids = jnp.concatenate([ids_of(y, c), ids_of(y, 1 - c)])
    near = jnp.concatenate([side, side2], axis=0)
    at = y + 1 - 2 * c
    at2 = y - 1 + 2 * c
    near_ids = jnp.concatenate([ids_of(at, c), ids_of(at2, 1 - c)])

    top1, total1, ps1, mix1, ch1 = part(own, queries, own_ids, positive, scale)
    top2, total2, ps2, mix2, ch2 = part(near, queries, near_ids, positive, scale)
    top = jnp.maximum(top1, top2)
    f1, f2 = jnp.exp(top1 - top), jnp.exp(top2 - top)
    stats = jnp.stack([top, total1 * f1 + total2 * f2, ps1 + ps2])
    n_outer = lax.axis_size(OUTER)
    copies = jnp.broadcast_to(stats, (n_outer, *stats.shape))
    every = lax.all_to_all(copies, OUTER, split_axis=0, concat_axis=0, tiled=True)
    top_all = jnp.max(every[:, 0], axis=0)
    total = jnp.sum(every[:, 1] * jnp.exp(every[:, 0] - top_all[None, :]), axis=0)
    pscore = jnp.sum(every[:, 2], axis=0)
    inv = jnp.exp(top - top_all) / total
    out = mix1 * (f1 * inv)[None, :] + mix2 * (f2 * inv)[None, :] - (ch1 + ch2)
    out = out.astype(jnp.bfloat16).reshape(n_outer, width // n_outer, count)
    got = lax.all_to_all(out, OUTER, split_axis=0, concat_axis=0, tiled=True)
    grad = scale * jnp.sum(got.astype(jnp.float32), axis=0)
    loss = top_all + jnp.log(total) - pscore
    return grad.astype(jnp.bfloat16).T, loss


def solution(mesh):
    devices = mesh.devices
    torus = Mesh(devices.reshape(4, 4, 8, 2, 2), ("yh", "x", "z", "yl", "c"))
    in_specs = (P(INNER, None), P((*OUTER, *INNER), None), P(INNER))
    out_specs = (P(INNER, OUTER), P(INNER))
    return jax.shard_map(
        shards, mesh=torus, in_specs=in_specs, out_specs=out_specs, check_vma=False
    )
```

```python
import functools
import math

import jax
import jax.numpy as jnp
from jax import lax
from jax.experimental import pallas as pl
from jax.experimental.pallas import tpu as pltpu
from jax.sharding import Mesh
from jax.sharding import PartitionSpec as P

INNER = ("z", "yl", "c")
OUTER = ("yh", "x")
LANE = ("yh", "yl", "c")
F32, BF16 = jnp.float32, jnp.bfloat16
VMEM = pl.BlockSpec(memory_space=pltpu.VMEM)
SMEM = pl.BlockSpec(memory_space=pltpu.SMEM)


def swapped(x):
    return lax.ppermute(x, "c", [(0, 1), (1, 0)])


def to_sides(x, ny):
    perm = []
    for y in range(ny):
        perm.append((2 * y, 2 * ((y - 1) % ny)))
        perm.append((2 * y + 1, 2 * ((y + 1) % ny) + 1))
    return lax.ppermute(x, LANE, perm)


def dot(a, b, dims):
    return lax.dot_general(a, b, (dims, ((), ())), preferred_element_type=F32)


def hits_of(pos_ref, base, count, rows):
    j = lax.broadcasted_iota(jnp.int32, (count, 1), 0)
    return (j // rows) * (4 * rows) + j % rows == pos_ref[...] - base


def statistics(p_refs, bases, q_ref, pos_ref, s_ref, scale, rows):
    q = q_ref[...]
    top = ps = None
    for i, p_ref in enumerate(p_refs):
        n = p_ref.shape[0]
        s = dot(p_ref[...], q, ((1,), (1,))) * scale
        s_ref[i * n : (i + 1) * n, :] = s
        hit = hits_of(pos_ref, bases[i], n, rows)
        t = jnp.max(s, axis=0, keepdims=True)
        u = jnp.sum(jnp.where(hit, s, 0.0), axis=0, keepdims=True)
        top = t if top is None else jnp.maximum(top, t)
        ps = u if ps is None else ps + u
    return top, ps


def products(p_refs, bases, w_ref, pos_ref, rows):
    mix = chosen = 0.0
    for i, p_ref in enumerate(p_refs):
        n = p_ref.shape[0]
        p = p_ref[...]
        hit = hits_of(pos_ref, bases[i], n, rows).astype(F32).astype(BF16)
        mix += dot(p, w_ref[i * n : (i + 1) * n, :], ((0,), (0,)))
        chosen += dot(p, hit, ((0,), (0,)))
    return mix, chosen


def own_kernel(scale, rows, base_ref, a_ref, b_ref, q_ref, pos_ref, st_ref, mix_ref, ch_ref, s_ref, w_ref):
    bases = (base_ref[0], base_ref[1])
    top, ps = statistics((a_ref, b_ref), bases, q_ref, pos_ref, s_ref, scale, rows)
    e = jnp.exp(s_ref[...] - top)
    w_ref[...] = e.astype(BF16)
    st_ref[0:1, :] = top
    st_ref[1:2, :] = jnp.sum(e, axis=0, keepdims=True)
    st_ref[2:3, :] = ps
    mix, chosen = products((a_ref, b_ref), bases, w_ref, pos_ref, rows)
    mix_ref[...] = mix
    ch_ref[...] = chosen.astype(BF16)


def side_kernel(scale, rows, base_ref, a_ref, q_ref, pos_ref, s_ref, st_ref):
    top, ps = statistics((a_ref,), (base_ref[2],), q_ref, pos_ref, s_ref, scale, rows)
    st_ref[0:1, :] = top
    st_ref[2:3, :] = ps


def last_kernel(scale, rows, base_ref, b_ref, q_ref, pos_ref, st1_ref, st2_ref, sa_ref, st_ref, w_ref, out_ref, s_ref):
    n = b_ref.shape[0]
    top3, ps = statistics((b_ref,), (base_ref[3],), q_ref, pos_ref, s_ref, scale, rows)
    top1 = st1_ref[0:1, :]
    top = jnp.maximum(jnp.maximum(top1, st2_ref[0:1, :]), top3)
    f1 = jnp.exp(top1 - top)
    total = st1_ref[1:2, :] * f1
    for i, piece in enumerate((sa_ref, s_ref)):
        e = jnp.exp(piece[...] - top)
        w_ref[i * n : (i + 1) * n, :] = e.astype(BF16)
        total += jnp.sum(e, axis=0, keepdims=True)
    ps += st1_ref[2:3, :] + st2_ref[2:3, :]
    st_ref[0:1, :] = top
    st_ref[1:2, :] = f1
    stats = jnp.concatenate([top, total, ps, ps], axis=0)
    out_ref[...] = jnp.broadcast_to(stats[None], out_ref.shape)


def near_kernel(rows, base_ref, a_ref, b_ref, w_ref, pos_ref, st_ref, mix_ref, ch_ref, m_ref, c_ref):
    bases = (base_ref[2], base_ref[3])
    mix, chosen = products((a_ref, b_ref), bases, w_ref, pos_ref, rows)
    m_ref[...] = mix + mix_ref[...] * st_ref[1:2, :]
    c_ref[...] = chosen + ch_ref[...].astype(F32)


def scale_kernel(every_ref, st_ref, m_ref, c_ref, out_ref, fin_ref):
    tops = every_ref[:, 0, :]
    top = jnp.max(tops, axis=0, keepdims=True)
    total = jnp.sum(every_ref[:, 1, :] * jnp.exp(tops - top), axis=0, keepdims=True)
    ps = jnp.sum(every_ref[:, 2, :], axis=0, keepdims=True)
    g = jnp.exp(st_ref[0:1, :] - top) / total
    out_ref[...] = (m_ref[...] * g - c_ref[...]).astype(BF16)
    fin_ref[0:1, :] = top
    fin_ref[1:2, :] = total
    fin_ref[2:3, :] = ps


def call(body, out, operands, scratch=(), flops=0, name=None, vmem=20):
    out_shape = [jax.ShapeDtypeStruct(s, d) for s, d in out]
    return pl.pallas_call(
        body,
        in_specs=[SMEM if o.dtype == jnp.int32 and o.ndim == 1 else VMEM for o in operands],
        out_specs=[VMEM] * len(out),
        out_shape=out_shape,
        scratch_shapes=[pltpu.VMEM(s, d) for s, d in scratch],
        cost_estimate=pl.CostEstimate(flops=flops, bytes_accessed=4 << 20, transcendentals=0),
        compiler_params=pltpu.CompilerParams(vmem_limit_bytes=vmem << 20),
        name=name,
    )(*operands)


def shards(queries, passages, positive):
    count, width = queries.shape
    rows = passages.shape[0]
    scale = 3.0 / math.sqrt(width)
    nz, nx = lax.axis_size("z"), lax.axis_size("x")
    ny = lax.axis_size("yh") * 2
    n_outer = lax.axis_size(OUTER)
    x, c = lax.axis_index("x"), lax.axis_index("c")
    y = lax.axis_index("yh") * 2 + lax.axis_index("yl")
    n = nz * rows
    flops = 2 * n * width * count

    def base_of(yy, cc):
        yy = (yy + ny) & (ny - 1)
        return ((((yy >> 1) * nx + x) * nz * 2 + (yy & 1)) * 2 + cc) * rows

    base = jnp.stack([base_of(y, c), base_of(y, 1 - c), base_of(y + 1 - 2 * c, c), base_of(y - 1 + 2 * c, 1 - c)])
    pos = positive.reshape(1, count)

    copies = jnp.broadcast_to(passages, (nz, rows, width))
    column = lax.all_to_all(copies, "z", split_axis=0, concat_axis=0, tiled=True)
    column = column.reshape(n, width)
    side = to_sides(column, ny)
    column2 = swapped(column)
    st1, mix1, ch1 = call(
        functools.partial(own_kernel, scale, rows),
        [((8, count), F32), ((width, count), F32), ((width, count), BF16)],
        (base, column, column2, queries, pos),
        [((2 * n, count), F32), ((2 * n, count), BF16)],
        6 * flops,
        "own",
    )
    side, st1 = lax.optimization_barrier((side, st1))
    side2 = swapped(side)
    scores, st2 = call(
        functools.partial(side_kernel, scale, rows),
        [((n, count), F32), ((8, count), F32)],
        (base, side, queries, pos),
        (),
        flops,
        "side",
    )
    st, weights, stats = call(
        functools.partial(last_kernel, scale, rows),
        [((8, count), F32), ((2 * n, count), BF16), ((n_outer, 4, count), F32)],
        (base, side2, queries, pos, st1, st2, scores),
        [((n, count), F32)],
        flops,
        "last",
    )
    every = lax.all_to_all(stats, OUTER, split_axis=0, concat_axis=0, tiled=True)
    m, ch = call(
        functools.partial(near_kernel, rows),
        [((width, count), F32), ((width, count), F32)],
        (base, side, side2, weights, pos, st, mix1, ch1),
        (),
        4 * flops,
        "near",
    )
    out, fin = call(
        scale_kernel,
        [((width, count), BF16), ((8, count), F32)],
        (every, st, m, ch),
        (),
        0,
        "scale",
    )
    out = out.reshape(n_outer, width // n_outer, count)
    got = lax.all_to_all(out, OUTER, split_axis=0, concat_axis=0, tiled=True)
    grad = scale * jnp.sum(got.astype(F32), axis=0)
    loss = fin[0] + jnp.log(fin[1]) - fin[2]
    return grad.astype(BF16).T, loss


def solution(mesh):
    devices = mesh.devices
    torus = Mesh(devices.reshape(4, 4, 8, 2, 2), ("yh", "x", "z", "yl", "c"))
    in_specs = (P(INNER, None), P((*OUTER, *INNER), None), P(INNER))
    out_specs = (P(INNER, OUTER), P(INNER))
    return jax.shard_map(
        shards, mesh=torus, in_specs=in_specs, out_specs=out_specs, check_vma=False
    )
```

```python
import functools
import math

import jax
import jax.numpy as jnp
from jax import lax
from jax.experimental import pallas as pl
from jax.experimental.pallas import tpu as pltpu
from jax.sharding import Mesh
from jax.sharding import PartitionSpec as P

INNER = ("z", "yl", "c")
OUTER = ("yh", "x")
LANE = ("yh", "yl", "c")
F32, BF16 = jnp.float32, jnp.bfloat16
VMEM = pl.BlockSpec(memory_space=pltpu.VMEM)
SMEM = pl.BlockSpec(memory_space=pltpu.SMEM)


def swapped(x):
    return lax.ppermute(x, "c", [(0, 1), (1, 0)])


def to_sides(x, ny):
    perm = []
    for y in range(ny):
        perm.append((2 * y, 2 * ((y - 1) % ny)))
        perm.append((2 * y + 1, 2 * ((y + 1) % ny) + 1))
    return lax.ppermute(x, LANE, perm)


def dot(a, b, dims):
    return lax.dot_general(a, b, (dims, ((), ())), preferred_element_type=F32)


def hits_of(pos_ref, base, count, rows):
    j = lax.broadcasted_iota(jnp.int32, (count, 1), 0)
    return (j // rows) * (4 * rows) + j % rows == pos_ref[...] - base


def statistics(p_refs, bases, q_ref, pos_ref, s_ref, scale, rows):
    q = q_ref[...]
    top = ps = None
    for i, p_ref in enumerate(p_refs):
        n = p_ref.shape[0]
        s = dot(p_ref[...], q, ((1,), (1,))) * scale
        s_ref[i * n : (i + 1) * n, :] = s
        hit = hits_of(pos_ref, bases[i], n, rows)
        t = jnp.max(s, axis=0, keepdims=True)
        u = jnp.sum(jnp.where(hit, s, 0.0), axis=0, keepdims=True)
        top = t if top is None else jnp.maximum(top, t)
        ps = u if ps is None else ps + u
    return top, ps


def products(p_refs, bases, w_ref, pos_ref, rows):
    mix = chosen = 0.0
    for i, p_ref in enumerate(p_refs):
        n = p_ref.shape[0]
        p = p_ref[...]
        hit = hits_of(pos_ref, bases[i], n, rows).astype(F32).astype(BF16)
        mix += dot(p, w_ref[i * n : (i + 1) * n, :], ((0,), (0,)))
        chosen += dot(p, hit, ((0,), (0,)))
    return mix, chosen


def flash(p_refs, bases, q_ref, pos_ref, s_ref, w_ref, scale, rows):
    top, ps = statistics(p_refs, bases, q_ref, pos_ref, s_ref, scale, rows)
    e = jnp.exp(s_ref[...] - top)
    w_ref[...] = e.astype(BF16)
    total = jnp.sum(e, axis=0, keepdims=True)
    mix, chosen = products(p_refs, bases, w_ref, pos_ref, rows)
    return top, total, ps, mix, chosen


def merged(st_ref, mix_ref, ch_ref, part):
    top, total, ps, mix, chosen = part
    both = jnp.maximum(st_ref[0:1, :], top)
    f, g = jnp.exp(st_ref[0:1, :] - both), jnp.exp(top - both)
    total = st_ref[1:2, :] * f + total * g
    ps += st_ref[2:3, :]
    return both, total, ps, mix_ref[...] * f + mix * g, ch_ref[...].astype(F32) + chosen


def put(refs, part):
    st_ref, mix_ref, ch_ref = refs
    top, total, ps, mix, chosen = part
    st_ref[0:1, :] = top
    st_ref[1:2, :] = total
    st_ref[2:3, :] = ps
    mix_ref[...] = mix
    ch_ref[...] = chosen.astype(BF16)


def own_kernel(scale, rows, base_ref, a_ref, b_ref, q_ref, pos_ref, st_ref, mix_ref, ch_ref, s_ref, w_ref):
    bases = (base_ref[0], base_ref[1])
    put((st_ref, mix_ref, ch_ref), flash((a_ref, b_ref), bases, q_ref, pos_ref, s_ref, w_ref, scale, rows))


def side_kernel(scale, rows, base_ref, a_ref, q_ref, pos_ref, st0_ref, mix0_ref, ch0_ref, st_ref, mix_ref, ch_ref, s_ref, w_ref):
    part = flash((a_ref,), (base_ref[2],), q_ref, pos_ref, s_ref, w_ref, scale, rows)
    put((st_ref, mix_ref, ch_ref), merged(st0_ref, mix0_ref, ch0_ref, part))


def split3(v):
    a = v.astype(BF16).astype(F32)
    b = (v - a).astype(BF16).astype(F32)
    return [a, b, v - a - b]


def stat_rows(top, total, ps):
    parts = split3(top) + split3(total) + split3(ps)
    parts.append(jnp.zeros((16 - len(parts), top.shape[1]), F32))
    return jnp.concatenate(parts, axis=0).astype(BF16)


def last_kernel(scale, rows, nx, base_ref, b_ref, q_ref, pos_ref, st0_ref, mix0_ref, ch0_ref, out_ref, s_ref, w_ref):
    part = flash((b_ref,), (base_ref[3],), q_ref, pos_ref, s_ref, w_ref, scale, rows)
    top, total, ps, mix, chosen = merged(st0_ref, mix0_ref, ch0_ref, part)
    mix, chosen = mix.astype(BF16), chosen.astype(BF16)
    stats = stat_rows(top, total, ps)
    width = mix.shape[0] // nx
    piece = width // 4
    for x in range(nx):
        for y in range(4):
            at = (y * nx + x) * piece
            out_ref[x, y * piece : (y + 1) * piece, :] = mix[at : at + piece]
            out_ref[x, width + y * piece : width + (y + 1) * piece, :] = chosen[at : at + piece]
        out_ref[x, 2 * width :, :] = stats


def combined(got_ref):
    n = got_ref.shape[0]
    width = (got_ref.shape[1] - 16) // 2
    stats = [got_ref[i, 2 * width :, :].astype(F32) for i in range(n)]
    three = [[s[3 * k : 3 * k + 1] + s[3 * k + 1 : 3 * k + 2] + s[3 * k + 2 : 3 * k + 3] for k in range(3)] for s in stats]
    top = functools.reduce(jnp.maximum, [t[0] for t in three])
    total = ps = mix = chosen = 0.0
    for i in range(n):
        f = jnp.exp(three[i][0] - top)
        total += three[i][1] * f
        ps += three[i][2]
        mix += got_ref[i, :width, :].astype(F32) * f
        chosen += got_ref[i, width : 2 * width, :].astype(F32)
    return top, total, ps, mix, chosen


def middle_kernel(got_ref, out_ref):
    top, total, ps, mix, chosen = combined(got_ref)
    mix, chosen = mix.astype(BF16), chosen.astype(BF16)
    stats = stat_rows(top, total, ps)
    n = out_ref.shape[0]
    piece = mix.shape[0] // n
    for y in range(n):
        out_ref[y, :piece, :] = mix[y * piece : (y + 1) * piece]
        out_ref[y, piece : 2 * piece, :] = chosen[y * piece : (y + 1) * piece]
        out_ref[y, 2 * piece :, :] = stats


def final_kernel(scale, got_ref, grad_ref, loss_ref):
    top, total, ps, mix, chosen = combined(got_ref)
    grad_ref[...] = (scale * (mix / total - chosen)).astype(BF16)
    loss_ref[...] = top + jnp.log(total) - ps


def call(body, out, operands, scratch=(), flops=0, name=None, vmem=20):
    out_shape = [jax.ShapeDtypeStruct(s, d) for s, d in out]
    return pl.pallas_call(
        body,
        in_specs=[SMEM if o.dtype == jnp.int32 and o.ndim == 1 else VMEM for o in operands],
        out_specs=[VMEM] * len(out),
        out_shape=out_shape,
        scratch_shapes=[pltpu.VMEM(s, d) for s, d in scratch],
        cost_estimate=pl.CostEstimate(flops=flops, bytes_accessed=4 << 20, transcendentals=0),
        compiler_params=pltpu.CompilerParams(vmem_limit_bytes=vmem << 20),
        name=name,
    )(*operands)


def shards(queries, passages, positive):
    count, width = queries.shape
    rows = passages.shape[0]
    scale = 3.0 / math.sqrt(width)
    nz, nx = lax.axis_size("z"), lax.axis_size("x")
    ny = lax.axis_size("yh") * 2
    x, c = lax.axis_index("x"), lax.axis_index("c")
    y = lax.axis_index("yh") * 2 + lax.axis_index("yl")
    n = nz * rows
    flops = 2 * n * width * count

    def base_of(yy, cc):
        yy = (yy + ny) & (ny - 1)
        return ((((yy >> 1) * nx + x) * nz * 2 + (yy & 1)) * 2 + cc) * rows

    base = jnp.stack([base_of(y, c), base_of(y, 1 - c), base_of(y + 1 - 2 * c, c), base_of(y - 1 + 2 * c, 1 - c)])
    pos = positive.reshape(1, count)

    copies = jnp.broadcast_to(passages, (nz, rows, width))
    column = lax.all_to_all(copies, "z", split_axis=0, concat_axis=0, tiled=True)
    column = column.reshape(n, width)
    side = to_sides(column, ny)
    column2 = swapped(column)
    st1, mix1, ch1 = call(
        functools.partial(own_kernel, scale, rows),
        [((8, count), F32), ((width, count), F32), ((width, count), BF16)],
        (base, column, column2, queries, pos),
        [((2 * n, count), F32), ((2 * n, count), BF16)],
        6 * flops,
        "own",
    )
    side, st1 = lax.optimization_barrier((side, st1))
    side2 = swapped(side)
    st2, mix2, ch2 = call(
        functools.partial(side_kernel, scale, rows),
        [((8, count), F32), ((width, count), F32), ((width, count), BF16)],
        (base, side, queries, pos, st1, mix1, ch1),
        [((n, count), F32), ((n, count), BF16)],
        3 * flops,
        "side",
    )
    nyh = ny // 2
    (out,) = call(
        functools.partial(last_kernel, scale, rows, nx),
        [((nx, 2 * width // nx + 16, count), BF16)],
        (base, side2, queries, pos, st2, mix2, ch2),
        [((n, count), F32), ((n, count), BF16)],
        3 * flops,
        "last",
    )
    got = lax.all_to_all(out, "x", split_axis=0, concat_axis=0, tiled=True)
    piece = width // (nx * nyh)
    (out,) = call(middle_kernel, [((nyh, 2 * piece + 16, count), BF16)], (got,), name="middle")
    got = lax.all_to_all(out, "yh", split_axis=0, concat_axis=0, tiled=True)
    grad, loss = call(
        functools.partial(final_kernel, scale),
        [((piece, count), BF16), ((1, count), F32)],
        (got,),
        name="final",
    )
    return grad.T, loss.reshape(count)


def solution(mesh):
    devices = mesh.devices
    torus = Mesh(devices.reshape(4, 4, 8, 2, 2), ("yh", "x", "z", "yl", "c"))
    in_specs = (P(INNER, None), P((*OUTER, *INNER), None), P(INNER))
    out_specs = (P(INNER, OUTER), P(INNER))
    return jax.shard_map(
        shards, mesh=torus, in_specs=in_specs, out_specs=out_specs, check_vma=False
    )
```

```python
import functools
import math

import jax
import jax.numpy as jnp
from jax import lax
from jax.experimental import pallas as pl
from jax.experimental.pallas import tpu as pltpu
from jax.sharding import Mesh
from jax.sharding import PartitionSpec as P


INNER = ("z", "yl", "c")
OUTER = ("yh", "x")
LANE = ("yh", "yl", "c")
F32, BF16 = jnp.float32, jnp.bfloat16
VMEM = pl.BlockSpec(memory_space=pltpu.VMEM)
SMEM = pl.BlockSpec(memory_space=pltpu.SMEM)


def swapped(x):
    return lax.ppermute(x, "c", [(0, 1), (1, 0)])


def to_sides(x, ny):
    perm = []
    for y in range(ny):
        perm.append((2 * y, 2 * ((y - 1) % ny)))
        perm.append((2 * y + 1, 2 * ((y + 1) % ny) + 1))
    return lax.ppermute(x, LANE, perm)


def dot(a, b, dims):
    return lax.dot_general(a, b, (dims, ((), ())), preferred_element_type=F32)


def hits_of(pos_ref, base, count, rows):
    j = lax.broadcasted_iota(jnp.int32, (count, 1), 0)
    return (j // rows) * (4 * rows) + j % rows == pos_ref[...] - base


def statistics(p_refs, bases, q_ref, pos_ref, s_ref, scale, rows):
    q = q_ref[...]
    top = ps = None
    for i, p_ref in enumerate(p_refs):
        n = p_ref.shape[0]
        s = dot(p_ref[...], q, ((1,), (1,))) * scale
        s_ref[i * n : (i + 1) * n, :] = s
        hit = hits_of(pos_ref, bases[i], n, rows)
        t = jnp.max(s, axis=0, keepdims=True)
        u = jnp.sum(jnp.where(hit, s, 0.0), axis=0, keepdims=True)
        top = t if top is None else jnp.maximum(top, t)
        ps = u if ps is None else ps + u
    return top, ps


def products(p_refs, bases, w_ref, pos_ref, rows):
    mix = chosen = 0.0
    for i, p_ref in enumerate(p_refs):
        n = p_ref.shape[0]
        p = p_ref[...]
        hit = hits_of(pos_ref, bases[i], n, rows).astype(F32).astype(BF16)
        mix += dot(p, w_ref[i * n : (i + 1) * n, :], ((0,), (0,)))
        chosen += dot(p, hit, ((0,), (0,)))
    return mix, chosen


def stat_kernel(scale, rows, base_ref, a_ref, b_ref, q_ref, pos_ref, qf_ref, posf_ref, st_ref, w_ref, out_ref, s_ref):
    bases = (base_ref[0], base_ref[1])
    pieces = []
    for qq, pp in ((qf_ref, posf_ref), (q_ref, pos_ref)):
        top, ps = statistics((a_ref, b_ref), bases, qq, pp, s_ref, scale, rows)
        e = jnp.exp(s_ref[...] - top)
        total = jnp.sum(e, axis=0, keepdims=True)
        pieces.append(jnp.concatenate([top, total, ps, ps], axis=0))
    st_ref[0:1, :] = top
    w_ref[...] = e.astype(BF16)
    theirs, own = pieces
    lower = base_ref[4] == 0
    half = out_ref.shape[0] // 2
    shape = (half, *own.shape)
    out_ref[:half] = jnp.broadcast_to(jnp.where(lower, own, theirs)[None], shape)
    out_ref[half:] = jnp.broadcast_to(jnp.where(lower, theirs, own)[None], shape)


def own_kernel(rows, base_ref, a_ref, b_ref, w_ref, pos_ref, mix_ref, ch_ref):
    mix, chosen = products((a_ref, b_ref), (base_ref[0], base_ref[1]), w_ref, pos_ref, rows)
    mix_ref[...] = mix
    ch_ref[...] = chosen.astype(BF16)


def near_kernel(scale, rows, base_ref, a_ref, b_ref, q_ref, pos_ref, st0_ref, mix0_ref, ch0_ref, st_ref, m_ref, c_ref, s_ref, w_ref):
    bases = (base_ref[2], base_ref[3])
    top, _ = statistics((a_ref, b_ref), bases, q_ref, pos_ref, s_ref, scale, rows)
    top0 = st0_ref[0:1, :]
    top = jnp.maximum(top, top0)
    w_ref[...] = jnp.exp(s_ref[...] - top).astype(BF16)
    mix, chosen = products((a_ref, b_ref), bases, w_ref, pos_ref, rows)
    st_ref[0:1, :] = top
    m_ref[...] = mix + mix0_ref[...] * jnp.exp(top0 - top)
    c_ref[...] = (chosen + ch0_ref[...].astype(F32)).astype(BF16)


def scale_kernel(every_ref, st_ref, m_ref, c_ref, out_ref, loss_ref):
    tops = every_ref[:, 0, :]
    top = jnp.max(tops, axis=0, keepdims=True)
    total = jnp.sum(every_ref[:, 1, :] * jnp.exp(tops - top), axis=0, keepdims=True)
    ps = jnp.sum(every_ref[:, 2, :], axis=0, keepdims=True)
    g = jnp.exp(st_ref[0:1, :] - top) / total
    out_ref[...] = (m_ref[...] * g - c_ref[...].astype(F32)).astype(BF16)
    loss_ref[...] = top + jnp.log(total) - ps


def final_kernel(scale, got_ref, grad_ref):
    total = got_ref[0].astype(F32)
    for i in range(1, got_ref.shape[0]):
        total += got_ref[i].astype(F32)
    grad_ref[...] = (scale * total).astype(BF16)


def call(body, out, operands, scratch=(), flops=0, vmem=20):
    out_shape = [jax.ShapeDtypeStruct(s, d) for s, d in out]
    return pl.pallas_call(
        body,
        in_specs=[SMEM if o.dtype == jnp.int32 and o.ndim == 1 else VMEM for o in operands],
        out_specs=[VMEM] * len(out),
        out_shape=out_shape,
        scratch_shapes=[pltpu.VMEM(s, d) for s, d in scratch],
        cost_estimate=pl.CostEstimate(flops=flops, bytes_accessed=4 << 20, transcendentals=0),
        compiler_params=pltpu.CompilerParams(vmem_limit_bytes=vmem << 20),
    )(*operands)


def shards(queries, passages, positive):
    count, width = queries.shape
    rows = passages.shape[0]
    scale = 3.0 / math.sqrt(width)
    nz, nx = lax.axis_size("z"), lax.axis_size("x")
    ny = lax.axis_size("yh") * 2
    x, c = lax.axis_index("x"), lax.axis_index("c")
    y = lax.axis_index("yh") * 2 + lax.axis_index("yl")
    n = nz * rows
    flops = 2 * n * width * count

    def base_of(yy, cc):
        yy = (yy + ny) & (ny - 1)
        return ((((yy >> 1) * nx + x) * nz * 2 + (yy & 1)) * 2 + cc) * rows

    base = jnp.stack(
        [base_of(y, c), base_of(y, 1 - c), base_of(y + 1 - 2 * c, c), base_of(y - 1 + 2 * c, 1 - c), y & 1]
    )
    pos = positive.reshape(1, count)

    theirs = to_sides(queries, ny)
    pos_theirs = to_sides(pos, ny)
    copies = jnp.broadcast_to(passages, (nz, rows, width))
    column = lax.all_to_all(copies, "z", split_axis=0, concat_axis=0, tiled=True)
    column, theirs, pos_theirs = lax.optimization_barrier((column, theirs, pos_theirs))
    column = column.reshape(n, width)
    side = to_sides(column, ny)
    column2 = swapped(column)
    members = ny * nx
    st1, weights, stats = call(
        functools.partial(stat_kernel, scale, rows),
        [((8, count), F32), ((2 * n, count), BF16), ((members, 4, count), F32)],
        (base, column, column2, queries, pos, theirs, pos_theirs),
        [((2 * n, count), F32)],
        4 * flops,
    )
    every = lax.all_to_all(stats, ("yl", *OUTER), split_axis=0, concat_axis=0, tiled=True)
    mix1, ch1 = call(
        functools.partial(own_kernel, rows),
        [((width, count), F32), ((width, count), BF16)],
        (base, column, column2, weights, pos),
        (),
        4 * flops,
    )
    side2 = swapped(side)
    st, m, ch = call(
        functools.partial(near_kernel, scale, rows),
        [((8, count), F32), ((width, count), F32), ((width, count), BF16)],
        (base, side, side2, queries, pos, st1, mix1, ch1),
        [((2 * n, count), F32), ((2 * n, count), BF16)],
        6 * flops,
    )
    out, loss = call(scale_kernel, [((width, count), BF16), ((1, count), F32)], (every, st, m, ch))
    n_outer = members // 2
    out = out.reshape(n_outer, width // n_outer, count)
    got = lax.all_to_all(out, OUTER, split_axis=0, concat_axis=0, tiled=True)
    (grad,) = call(
        functools.partial(final_kernel, scale), [((width // n_outer, count), BF16)], (got,)
    )
    return grad.T, loss.reshape(count)


def solution(mesh):
    devices = mesh.devices
    torus = Mesh(devices.reshape(4, 4, 8, 2, 2), ("yh", "x", "z", "yl", "c"))
    in_specs = (P(INNER, None), P((*OUTER, *INNER), None), P(INNER))
    out_specs = (P(INNER, OUTER), P(INNER))
    return jax.shard_map(
        shards, mesh=torus, in_specs=in_specs, out_specs=out_specs, check_vma=False
    )
```

```python
import functools
import math

import jax
import jax.numpy as jnp
from jax import lax
from jax.experimental import pallas as pl
from jax.experimental.pallas import tpu as pltpu
from jax.sharding import Mesh
from jax.sharding import PartitionSpec as P


INNER = ("z", "yl", "c")
OUTER = ("yh", "x")
LANE = ("yh", "yl", "c")
F32, BF16 = jnp.float32, jnp.bfloat16
VMEM = pl.BlockSpec(memory_space=pltpu.VMEM)
SMEM = pl.BlockSpec(memory_space=pltpu.SMEM)
HBM = pl.BlockSpec(memory_space=pltpu.HBM)


def swapped(x):
    return lax.ppermute(x, "c", [(0, 1), (1, 0)])


def to_sides(x, ny):
    perm = []
    for y in range(ny):
        perm.append((2 * y, 2 * ((y - 1) % ny)))
        perm.append((2 * y + 1, 2 * ((y + 1) % ny) + 1))
    return lax.ppermute(x, LANE, perm)


def dot(a, b, dims):
    return lax.dot_general(a, b, (dims, ((), ())), preferred_element_type=F32)


def hits_of(pos_ref, base, count, rows):
    j = lax.broadcasted_iota(jnp.int32, (count, 1), 0)
    return (j // rows) * (4 * rows) + j % rows == pos_ref[...] - base


def statistics(p_refs, bases, q_ref, pos_ref, s_ref, scale, rows):
    q = q_ref[...]
    top = ps = None
    for i, p_ref in enumerate(p_refs):
        n = p_ref.shape[0]
        s = dot(p_ref[...], q, ((1,), (1,))) * scale
        s_ref[i * n : (i + 1) * n, :] = s
        hit = hits_of(pos_ref, bases[i], n, rows)
        t = jnp.max(s, axis=0, keepdims=True)
        u = jnp.sum(jnp.where(hit, s, 0.0), axis=0, keepdims=True)
        top = t if top is None else jnp.maximum(top, t)
        ps = u if ps is None else ps + u
    return top, ps


def products(p_refs, bases, w_ref, pos_ref, rows):
    mix = chosen = 0.0
    for i, p_ref in enumerate(p_refs):
        n = p_ref.shape[0]
        p = p_ref[...]
        hit = hits_of(pos_ref, bases[i], n, rows).astype(F32).astype(BF16)
        mix += dot(p, w_ref[i * n : (i + 1) * n, :], ((0,), (0,)))
        chosen += dot(p, hit, ((0,), (0,)))
    return mix, chosen


def stat_kernel(scale, rows, base_ref, a_ref, b_ref, q_ref, pos_ref, qf_ref, posf_ref, st_ref, w_hbm, out_ref, s_ref, w_ref, sem):
    bases = (base_ref[0], base_ref[1])
    pieces = []
    for qq, pp in ((q_ref, pos_ref), (qf_ref, posf_ref)):
        top, ps = statistics((a_ref, b_ref), bases, qq, pp, s_ref, scale, rows)
        e = jnp.exp(s_ref[...] - top)
        total = jnp.sum(e, axis=0, keepdims=True)
        if not pieces:
            w_ref[...] = e.astype(BF16)
            copy = pltpu.make_async_copy(w_ref, w_hbm, sem)
            copy.start()
            st_ref[0:1, :] = top
        pieces.append(jnp.concatenate([top, total, ps, ps], axis=0))
    own, theirs = pieces
    lower = base_ref[4] == 0
    half = out_ref.shape[0] // 2
    shape = (half, *own.shape)
    out_ref[:half] = jnp.broadcast_to(jnp.where(lower, own, theirs)[None], shape)
    out_ref[half:] = jnp.broadcast_to(jnp.where(lower, theirs, own)[None], shape)
    copy.wait()


def own_kernel(rows, base_ref, a_hbm, b_hbm, w_hbm, pos_ref, mix_ref, ch_ref, a_ref, b_ref, w_ref, sems):
    pairs = ((a_hbm, a_ref), (b_hbm, b_ref), (w_hbm, w_ref))
    copies = [pltpu.make_async_copy(src, dst, sems.at[i]) for i, (src, dst) in enumerate(pairs)]
    for copy in copies:
        copy.start()
    n = a_ref.shape[0]
    chosen = 0.0
    for i, p_ref in enumerate((a_ref, b_ref)):
        hit = hits_of(pos_ref, base_ref[i], n, rows).astype(F32).astype(BF16)
        copies[i].wait()
        chosen += dot(p_ref[...], hit, ((0,), (0,)))
    ch_ref[...] = chosen.astype(BF16)
    copies[2].wait()
    mix_ref[...] = dot(a_ref[...], w_ref[:n, :], ((0,), (0,))) + dot(b_ref[...], w_ref[n:, :], ((0,), (0,)))


def near_kernel(scale, rows, base_ref, a_hbm, b_ref, q_ref, pos_ref, st0_ref, mix0_ref, ch0_ref, st_ref, m_ref, c_ref, s_ref, w_ref, a_ref, sem):
    copy = pltpu.make_async_copy(a_hbm, a_ref, sem)
    copy.start()
    bases = (base_ref[3], base_ref[2])
    q = q_ref[...]
    n = b_ref.shape[0]
    s_ref[:n, :] = dot(b_ref[...], q, ((1,), (1,))) * scale
    copy.wait()
    s_ref[n:, :] = dot(a_ref[...], q, ((1,), (1,))) * scale
    top0 = st0_ref[0:1, :]
    top = jnp.maximum(jnp.max(s_ref[...], axis=0, keepdims=True), top0)
    w_ref[...] = jnp.exp(s_ref[...] - top).astype(BF16)
    mix, chosen = products((b_ref, a_ref), bases, w_ref, pos_ref, rows)
    st_ref[0:1, :] = top
    m_ref[...] = mix + mix0_ref[...] * jnp.exp(top0 - top)
    c_ref[...] = (chosen + ch0_ref[...].astype(F32)).astype(BF16)


def scale_kernel(every_ref, st_ref, m_ref, c_ref, out_ref, loss_ref):
    tops = every_ref[:, 0, :]
    top = jnp.max(tops, axis=0, keepdims=True)
    total = jnp.sum(every_ref[:, 1, :] * jnp.exp(tops - top), axis=0, keepdims=True)
    ps = jnp.sum(every_ref[:, 2, :], axis=0, keepdims=True)
    g = jnp.exp(st_ref[0:1, :] - top) / total
    out_ref[...] = (m_ref[...] * g - c_ref[...].astype(F32)).astype(BF16)
    loss_ref[...] = top + jnp.log(total) - ps


def final_kernel(scale, got_ref, grad_ref):
    total = got_ref[0].astype(F32)
    for i in range(1, got_ref.shape[0]):
        total += got_ref[i].astype(F32)
    grad_ref[...] = (scale * total).astype(BF16)


def call(body, out, operands, scratch=(), flops=0, vmem=12, hbm_in=(), hbm_out=()):
    def spec(i, o):
        if i in hbm_in:
            return HBM
        return SMEM if o.dtype == jnp.int32 and o.ndim == 1 else VMEM

    kernel = pl.pallas_call(
        body,
        in_specs=[spec(i, o) for i, o in enumerate(operands)],
        out_specs=[HBM if i in hbm_out else VMEM for i in range(len(out))],
        out_shape=[pltpu.HBM(s, d) if i in hbm_out else jax.ShapeDtypeStruct(s, d) for i, (s, d) in enumerate(out)],
        scratch_shapes=[s if not isinstance(s, tuple) else pltpu.VMEM(*s) for s in scratch],
        cost_estimate=pl.CostEstimate(flops=flops, bytes_accessed=4 << 20, transcendentals=0),
        compiler_params=pltpu.CompilerParams(vmem_limit_bytes=vmem << 20),
    )
    operands = [pltpu.with_memory_space_constraint(o, pltpu.HBM) if i in hbm_in else o for i, o in enumerate(operands)]
    return kernel(*operands)


def shards(queries, passages, positive):
    count, width = queries.shape
    rows = passages.shape[0]
    scale = 3.0 / math.sqrt(width)
    nz, nx = lax.axis_size("z"), lax.axis_size("x")
    ny = lax.axis_size("yh") * 2
    x, c = lax.axis_index("x"), lax.axis_index("c")
    y = lax.axis_index("yh") * 2 + lax.axis_index("yl")
    n = nz * rows
    flops = 2 * n * width * count

    def base_of(yy, cc):
        yy = (yy + ny) & (ny - 1)
        return ((((yy >> 1) * nx + x) * nz * 2 + (yy & 1)) * 2 + cc) * rows

    base = jnp.stack(
        [base_of(y, c), base_of(y, 1 - c), base_of(y + 1 - 2 * c, c), base_of(y - 1 + 2 * c, 1 - c), y & 1]
    )
    pos = positive.reshape(1, count)

    theirs = to_sides(queries, ny)
    pos_theirs = to_sides(pos, ny)
    copies = jnp.broadcast_to(passages, (nz, rows, width))
    column = lax.all_to_all(copies, "z", split_axis=0, concat_axis=0, tiled=True)
    column, theirs, pos_theirs = lax.optimization_barrier((column, theirs, pos_theirs))
    column = column.reshape(n, width)
    side = to_sides(column, ny)
    column2 = swapped(column)
    members = ny * nx
    st1, weights, stats = call(
        functools.partial(stat_kernel, scale, rows),
        [((8, count), F32), ((2 * n, count), BF16), ((members, 4, count), F32)],
        (base, column, column2, queries, pos, theirs, pos_theirs),
        [((2 * n, count), F32), ((2 * n, count), BF16), pltpu.SemaphoreType.DMA],
        4 * flops,
        hbm_out=(1,),
    )
    every = lax.all_to_all(stats, ("yl", *OUTER), split_axis=0, concat_axis=0, tiled=True)
    mix1, ch1 = call(
        functools.partial(own_kernel, rows),
        [((width, count), F32), ((width, count), BF16)],
        (base, column, column2, weights, pos),
        [((n, width), BF16), ((n, width), BF16), ((2 * n, count), BF16), pltpu.SemaphoreType.DMA((3,))],
        4 * flops,
        hbm_in=(1, 2, 3),
    )
    side2 = swapped(side)
    st, m, ch = call(
        functools.partial(near_kernel, scale, rows),
        [((8, count), F32), ((width, count), F32), ((width, count), BF16)],
        (base, side, side2, queries, pos, st1, mix1, ch1),
        [((2 * n, count), F32), ((2 * n, count), BF16), ((n, width), BF16), pltpu.SemaphoreType.DMA],
        6 * flops,
        hbm_in=(1,),
    )
    out, loss = call(scale_kernel, [((width, count), BF16), ((1, count), F32)], (every, st, m, ch))
    n_outer = members // 2
    out = out.reshape(n_outer, width // n_outer, count)
    got = lax.all_to_all(out, OUTER, split_axis=0, concat_axis=0, tiled=True)
    (grad,) = call(functools.partial(final_kernel, scale), [((width // n_outer, count), BF16)], (got,))
    return grad.T, loss.reshape(count)


def solution(mesh):
    devices = mesh.devices
    torus = Mesh(devices.reshape(4, 4, 8, 2, 2), ("yh", "x", "z", "yl", "c"))
    in_specs = (P(INNER, None), P((*OUTER, *INNER), None), P(INNER))
    out_specs = (P(INNER, OUTER), P(INNER))
    return jax.shard_map(shards, mesh=torus, in_specs=in_specs, out_specs=out_specs, check_vma=False)
```

```python
import functools
import math

import jax
import jax.numpy as jnp
from jax import lax
from jax.experimental import pallas as pl
from jax.experimental.pallas import tpu as pltpu
from jax.sharding import Mesh
from jax.sharding import PartitionSpec as P


INNER = ("z", "yl", "c")
OUTER = ("yh", "x")
LANE = ("yh", "yl", "c")
F32, BF16 = jnp.float32, jnp.bfloat16
LOG2E = math.log2(math.e)
VMEM = pl.BlockSpec(memory_space=pltpu.VMEM)
SMEM = pl.BlockSpec(memory_space=pltpu.SMEM)
HBM = pl.BlockSpec(memory_space=pltpu.HBM)


def swapped(x):
    return lax.ppermute(x, "c", [(0, 1), (1, 0)])


def to_sides(x, ny):
    perm = []
    for y in range(ny):
        perm.append((2 * y, 2 * ((y - 1) % ny)))
        perm.append((2 * y + 1, 2 * ((y + 1) % ny) + 1))
    return lax.ppermute(x, LANE, perm)


def dot(a, b, dims):
    return lax.dot_general(a, b, (dims, ((), ())), preferred_element_type=F32)


def hits_of(pos_ref, base, count, rows):
    j = lax.broadcasted_iota(jnp.int32, (count, 1), 0)
    return (j // rows) * (4 * rows) + j % rows == pos_ref[...] - base


def statistics(p_refs, bases, q_ref, pos_ref, s_ref, rows):
    q = q_ref[...]
    top = ps = None
    for i, p_ref in enumerate(p_refs):
        n = p_ref.shape[0]
        s = dot(p_ref[...], q, ((1,), (1,)))
        s_ref[i * n : (i + 1) * n, :] = s
        hit = hits_of(pos_ref, bases[i], n, rows)
        t = jnp.max(s, axis=0, keepdims=True)
        u = jnp.sum(jnp.where(hit, s, 0.0), axis=0, keepdims=True)
        top = t if top is None else jnp.maximum(top, t)
        ps = u if ps is None else ps + u
    return top, ps


def products(p_refs, bases, w_ref, pos_ref, rows):
    mix = chosen = 0.0
    for i, p_ref in enumerate(p_refs):
        n = p_ref.shape[0]
        p = p_ref[...]
        hit = hits_of(pos_ref, bases[i], n, rows).astype(F32).astype(BF16)
        mix += dot(p, w_ref[i * n : (i + 1) * n, :], ((0,), (0,)))
        chosen += dot(p, hit, ((0,), (0,)))
    return mix, chosen


def stat_kernel(scale, rows, base_ref, a_ref, b_ref, q_ref, pos_ref, qf_ref, posf_ref, st_ref, w_hbm, out_ref, s_ref, w_ref, sem):
    bases = (base_ref[0], base_ref[1])
    pieces = []
    for qq, pp in ((q_ref, pos_ref), (qf_ref, posf_ref)):
        top, ps = statistics((a_ref, b_ref), bases, qq, pp, s_ref, rows)
        e = jnp.exp2((s_ref[...] - top) * (scale * LOG2E))
        total = jnp.sum(e, axis=0, keepdims=True)
        if not pieces:
            w_ref[...] = e.astype(BF16)
            copy = pltpu.make_async_copy(w_ref, w_hbm, sem)
            copy.start()
            st_ref[0:1, :] = top
        pieces.append(jnp.concatenate([top * scale + jnp.log(total), ps * scale], axis=1))
    own, theirs = pieces
    lower = base_ref[4] == 0
    half = out_ref.shape[0] // 2
    shape = (half, *own.shape)
    out_ref[:half] = jnp.broadcast_to(jnp.where(lower, own, theirs)[None], shape)
    out_ref[half:] = jnp.broadcast_to(jnp.where(lower, theirs, own)[None], shape)
    copy.wait()


def own_kernel(rows, base_ref, a_hbm, b_hbm, w_hbm, pos_ref, mix_ref, ch_ref, a_ref, b_ref, w_ref, sems):
    pairs = ((a_hbm, a_ref), (b_hbm, b_ref), (w_hbm, w_ref))
    copies = [pltpu.make_async_copy(src, dst, sems.at[i]) for i, (src, dst) in enumerate(pairs)]
    for copy in copies:
        copy.start()
    n = a_ref.shape[0]
    chosen = 0.0
    for i, p_ref in enumerate((a_ref, b_ref)):
        hit = hits_of(pos_ref, base_ref[i], n, rows).astype(F32).astype(BF16)
        copies[i].wait()
        chosen += dot(p_ref[...], hit, ((0,), (0,)))
    ch_ref[...] = chosen.astype(BF16)
    copies[2].wait()
    mix_ref[...] = dot(a_ref[...], w_ref[:n, :], ((0,), (0,))) + dot(b_ref[...], w_ref[n:, :], ((0,), (0,)))


def near_kernel(scale, rows, base_ref, a_hbm, b_ref, q_ref, pos_ref, st0_ref, mix0_ref, ch0_ref, st_ref, m_ref, c_ref, s_ref, w_ref, a_ref, sem):
    copy = pltpu.make_async_copy(a_hbm, a_ref, sem)
    copy.start()
    bases = (base_ref[3], base_ref[2])
    q = q_ref[...]
    n = b_ref.shape[0]
    s_ref[:n, :] = dot(b_ref[...], q, ((1,), (1,)))
    copy.wait()
    s_ref[n:, :] = dot(a_ref[...], q, ((1,), (1,)))
    top0 = st0_ref[0:1, :]
    top = jnp.maximum(jnp.max(s_ref[...], axis=0, keepdims=True), top0)
    w_ref[...] = jnp.exp2((s_ref[...] - top) * (scale * LOG2E)).astype(BF16)
    mix, chosen = products((b_ref, a_ref), bases, w_ref, pos_ref, rows)
    st_ref[0:1, :] = top
    m_ref[...] = mix + mix0_ref[...] * jnp.exp2((top0 - top) * (scale * LOG2E))
    c_ref[...] = (chosen + ch0_ref[...].astype(F32)).astype(BF16)


def scale_kernel(scale, every_ref, st_ref, m_ref, c_ref, out_ref, loss_ref):
    count = m_ref.shape[1]
    lse = every_ref[:, 0, :count]
    most = jnp.max(lse, axis=0, keepdims=True)
    whole = most + jnp.log(jnp.sum(jnp.exp(lse - most), axis=0, keepdims=True))
    ps = jnp.sum(every_ref[:, 0, count:], axis=0, keepdims=True)
    g = jnp.exp(st_ref[0:1, :] * scale - whole)
    out_ref[...] = (m_ref[...] * g - c_ref[...].astype(F32)).astype(BF16)
    loss_ref[...] = whole - ps


def copy_kernel(x_ref, out_hbm, sems):
    n = out_hbm.shape[0]
    copies = [pltpu.make_async_copy(x_ref, out_hbm.at[i], sems.at[i]) for i in range(n)]
    for copy in copies:
        copy.start()
    for copy in copies:
        copy.wait()


def final_kernel(scale, got_ref, grad_ref):
    total = got_ref[0].astype(F32)
    for i in range(1, got_ref.shape[0]):
        total += got_ref[i].astype(F32)
    grad_ref[...] = (scale * total).astype(BF16)


def call(body, out, operands, scratch=(), flops=0, vmem=12, hbm_in=(), hbm_out=()):
    def spec(i, o):
        if i in hbm_in:
            return HBM
        return SMEM if o.dtype == jnp.int32 and o.ndim == 1 else VMEM

    kernel = pl.pallas_call(
        body,
        in_specs=[spec(i, o) for i, o in enumerate(operands)],
        out_specs=[HBM if i in hbm_out else VMEM for i in range(len(out))],
        out_shape=[pltpu.HBM(s, d) if i in hbm_out else jax.ShapeDtypeStruct(s, d) for i, (s, d) in enumerate(out)],
        scratch_shapes=[s if not isinstance(s, tuple) else pltpu.VMEM(*s) for s in scratch],
        cost_estimate=pl.CostEstimate(flops=flops, bytes_accessed=4 << 20, transcendentals=0),
        compiler_params=pltpu.CompilerParams(vmem_limit_bytes=vmem << 20),
    )
    operands = [pltpu.with_memory_space_constraint(o, pltpu.HBM) if i in hbm_in else o for i, o in enumerate(operands)]
    return kernel(*operands)


def shards(queries, passages, positive):
    count, width = queries.shape
    rows = passages.shape[0]
    scale = 3.0 / math.sqrt(width)
    nz, nx = lax.axis_size("z"), lax.axis_size("x")
    ny = lax.axis_size("yh") * 2
    x, c = lax.axis_index("x"), lax.axis_index("c")
    y = lax.axis_index("yh") * 2 + lax.axis_index("yl")
    n = nz * rows
    flops = 2 * n * width * count

    def base_of(yy, cc):
        yy = (yy + ny) & (ny - 1)
        return ((((yy >> 1) * nx + x) * nz * 2 + (yy & 1)) * 2 + cc) * rows

    base = jnp.stack(
        [base_of(y, c), base_of(y, 1 - c), base_of(y + 1 - 2 * c, c), base_of(y - 1 + 2 * c, 1 - c), y & 1]
    )
    pos = positive.reshape(1, count)

    theirs = to_sides(queries, ny)
    pos_theirs = to_sides(pos, ny)
    (copies,) = call(
        copy_kernel, [((nz, rows, width), BF16)], (passages,), [pltpu.SemaphoreType.DMA((nz,))], hbm_out=(0,)
    )
    column = lax.all_to_all(copies, "z", split_axis=0, concat_axis=0, tiled=True)
    column, theirs, pos_theirs = lax.optimization_barrier((column, theirs, pos_theirs))
    column = column.reshape(n, width)
    side = to_sides(column, ny)
    column2 = swapped(column)
    members = ny * nx
    st1, weights, stats = call(
        functools.partial(stat_kernel, scale, rows),
        [((8, count), F32), ((2 * n, count), BF16), ((members, 1, 2 * count), F32)],
        (base, column, column2, queries, pos, theirs, pos_theirs),
        [((2 * n, count), F32), ((2 * n, count), BF16), pltpu.SemaphoreType.DMA],
        4 * flops,
        hbm_out=(1,),
    )
    every = lax.all_to_all(stats, ("yl", *OUTER), split_axis=0, concat_axis=0, tiled=True)
    mix1, ch1 = call(
        functools.partial(own_kernel, rows),
        [((width, count), F32), ((width, count), BF16)],
        (base, column, column2, weights, pos),
        [((n, width), BF16), ((n, width), BF16), ((2 * n, count), BF16), pltpu.SemaphoreType.DMA((3,))],
        4 * flops,
        hbm_in=(1, 2, 3),
    )
    side2 = swapped(side)
    st, m, ch = call(
        functools.partial(near_kernel, scale, rows),
        [((8, count), F32), ((width, count), F32), ((width, count), BF16)],
        (base, side, side2, queries, pos, st1, mix1, ch1),
        [((2 * n, count), F32), ((2 * n, count), BF16), ((n, width), BF16), pltpu.SemaphoreType.DMA],
        6 * flops,
        hbm_in=(1,),
    )
    out, loss = call(
        functools.partial(scale_kernel, scale), [((width, count), BF16), ((1, count), F32)], (every, st, m, ch)
    )
    n_outer = members // 2
    out = out.reshape(n_outer, width // n_outer, count)
    got = lax.all_to_all(out, OUTER, split_axis=0, concat_axis=0, tiled=True)
    (grad,) = call(functools.partial(final_kernel, scale), [((width // n_outer, count), BF16)], (got,))
    return grad.T, loss.reshape(count)


def solution(mesh):
    devices = mesh.devices
    torus = Mesh(devices.reshape(4, 4, 8, 2, 2), ("yh", "x", "z", "yl", "c"))
    in_specs = (P(INNER, None), P((*OUTER, *INNER), None), P(INNER))
    out_specs = (P(INNER, OUTER), P(INNER))
    return jax.shard_map(shards, mesh=torus, in_specs=in_specs, out_specs=out_specs, check_vma=False)
```

```python
import functools
import math

import jax
import jax.numpy as jnp
from jax import lax
from jax.experimental import pallas as pl
from jax.experimental.pallas import tpu as pltpu
from jax.sharding import Mesh
from jax.sharding import PartitionSpec as P


INNER = ("z", "yl", "c")
OUTER = ("yh", "x")
LANE = ("yh", "yl", "c")
F32, BF16 = jnp.float32, jnp.bfloat16
LOG2E = math.log2(math.e)
VMEM = pl.BlockSpec(memory_space=pltpu.VMEM)
SMEM = pl.BlockSpec(memory_space=pltpu.SMEM)
HBM = pl.BlockSpec(memory_space=pltpu.HBM)


def swapped(x):
    return lax.ppermute(x, "c", [(0, 1), (1, 0)])


def to_sides(x, ny):
    perm = []
    for y in range(ny):
        perm.append((2 * y, 2 * ((y - 1) % ny)))
        perm.append((2 * y + 1, 2 * ((y + 1) % ny) + 1))
    return lax.ppermute(x, LANE, perm)


def dot(a, b, dims):
    return lax.dot_general(a, b, (dims, ((), ())), preferred_element_type=F32)


def hits_of(pos_ref, base, count, rows):
    j = lax.broadcasted_iota(jnp.int32, (count, 1), 0)
    return (j // rows) * (4 * rows) + j % rows == pos_ref[...] - base


def statistics(p_refs, bases, q_ref, pos_ref, s_ref, rows):
    q = q_ref[...]
    top = ps = None
    for i, p_ref in enumerate(p_refs):
        n = p_ref.shape[0]
        s = dot(p_ref[...], q, ((1,), (1,)))
        s_ref[i * n : (i + 1) * n, :] = s
        hit = hits_of(pos_ref, bases[i], n, rows)
        t = jnp.max(s, axis=0, keepdims=True)
        u = jnp.sum(jnp.where(hit, s, 0.0), axis=0, keepdims=True)
        top = t if top is None else jnp.maximum(top, t)
        ps = u if ps is None else ps + u
    return top, ps


def products(p_refs, bases, w_ref, pos_ref, rows):
    mix = chosen = 0.0
    for i, p_ref in enumerate(p_refs):
        n = p_ref.shape[0]
        p = p_ref[...]
        hit = hits_of(pos_ref, bases[i], n, rows).astype(F32).astype(BF16)
        mix += dot(p, w_ref[i * n : (i + 1) * n, :], ((0,), (0,)))
        chosen += dot(p, hit, ((0,), (0,)))
    return mix, chosen


def stat_kernel(scale, rows, base_ref, a_ref, b_ref, q_ref, pos_ref, qf_ref, posf_ref, st_ref, w_hbm, out_ref, s_ref, w_ref, sem):
    bases = (base_ref[0], base_ref[1])
    pieces = []
    for qq, pp in ((q_ref, pos_ref), (qf_ref, posf_ref)):
        top, ps = statistics((a_ref, b_ref), bases, qq, pp, s_ref, rows)
        e = jnp.exp2((s_ref[...] - top) * (scale * LOG2E))
        total = jnp.sum(e, axis=0, keepdims=True)
        if not pieces:
            w_ref[...] = e.astype(BF16)
            copy = pltpu.make_async_copy(w_ref, w_hbm, sem)
            copy.start()
            st_ref[0:1, :] = top
        pieces.append(jnp.concatenate([top * scale + jnp.log(total), ps * scale], axis=1))
    own, theirs = pieces
    lower = base_ref[4] == 0
    half = out_ref.shape[0] // 2
    shape = (half, *own.shape)
    out_ref[:half] = jnp.broadcast_to(jnp.where(lower, own, theirs)[None], shape)
    out_ref[half:] = jnp.broadcast_to(jnp.where(lower, theirs, own)[None], shape)
    copy.wait()


def load_kernel(*refs):
    count = (len(refs) - 1) // 2
    copies = [pltpu.make_async_copy(refs[i], refs[count + i], refs[-1].at[i]) for i in range(count)]
    for copy in copies:
        copy.start()
    for copy in copies:
        copy.wait()


def mix_kernel(scale, rows, base_ref, a_hbm, b_hbm, wo_hbm, side_ref, side2_ref, q_ref, pos_ref, st0_ref, st_ref, m_ref, c_ref, s_ref, w_ref, a_ref, b_ref, wo_ref, sems):
    pairs = ((a_hbm, a_ref), (b_hbm, b_ref), (wo_hbm, wo_ref))
    copies = [pltpu.make_async_copy(src, dst, sems.at[i]) for i, (src, dst) in enumerate(pairs)]
    for copy in copies:
        copy.start()
    q = q_ref[...]
    n = side2_ref.shape[0]
    s_ref[:n, :] = dot(side2_ref[...], q, ((1,), (1,)))
    s_ref[n:, :] = dot(side_ref[...], q, ((1,), (1,)))
    top0 = st0_ref[0:1, :]
    top = jnp.maximum(jnp.max(s_ref[...], axis=0, keepdims=True), top0)
    w_ref[...] = jnp.exp2((s_ref[...] - top) * (scale * LOG2E)).astype(BF16)
    st_ref[0:1, :] = top
    mix, chosen = products((side2_ref, side_ref), (base_ref[3], base_ref[2]), w_ref, pos_ref, rows)
    m_ref[...] = mix
    for copy in copies:
        copy.wait()
    mix, more = products((a_ref, b_ref), (base_ref[0], base_ref[1]), wo_ref, pos_ref, rows)
    m_ref[...] += mix * jnp.exp2((top0 - top) * (scale * LOG2E))
    c_ref[...] = (chosen + more).astype(BF16)


def scale_kernel(scale, every_ref, st_ref, m_ref, c_ref, out_ref, loss_ref):
    count = m_ref.shape[1]
    lse = every_ref[:, 0, :count]
    most = jnp.max(lse, axis=0, keepdims=True)
    whole = most + jnp.log(jnp.sum(jnp.exp(lse - most), axis=0, keepdims=True))
    ps = jnp.sum(every_ref[:, 0, count:], axis=0, keepdims=True)
    g = jnp.exp(st_ref[0:1, :] * scale - whole)
    out_ref[...] = (m_ref[...] * g - c_ref[...].astype(F32)).astype(BF16)
    loss_ref[...] = whole - ps


def copy_kernel(x_hbm, out_hbm, x_ref, sems):
    n = out_hbm.shape[0]
    first = pltpu.make_async_copy(x_hbm, x_ref, sems.at[n])
    first.start()
    first.wait()
    copies = [pltpu.make_async_copy(x_ref, out_hbm.at[i], sems.at[i]) for i in range(n)]
    for copy in copies:
        copy.start()
    for copy in copies:
        copy.wait()


def final_kernel(scale, got_ref, grad_ref):
    total = got_ref[0].astype(F32)
    for i in range(1, got_ref.shape[0]):
        total += got_ref[i].astype(F32)
    grad_ref[...] = (scale * total).astype(BF16)


def call(body, out, operands, scratch=(), flops=0, vmem=12, hbm_in=(), hbm_out=()):
    def spec(i, o):
        if i in hbm_in:
            return HBM
        return SMEM if o.dtype == jnp.int32 and o.ndim == 1 else VMEM

    kernel = pl.pallas_call(
        body,
        in_specs=[spec(i, o) for i, o in enumerate(operands)],
        out_specs=[HBM if i in hbm_out else VMEM for i in range(len(out))],
        out_shape=[pltpu.HBM(s, d) if i in hbm_out else jax.ShapeDtypeStruct(s, d) for i, (s, d) in enumerate(out)],
        scratch_shapes=[s if not isinstance(s, tuple) else pltpu.VMEM(*s) for s in scratch],
        cost_estimate=pl.CostEstimate(flops=flops, bytes_accessed=4 << 20, transcendentals=0),
        compiler_params=pltpu.CompilerParams(vmem_limit_bytes=vmem << 20),
    )
    operands = [pltpu.with_memory_space_constraint(o, pltpu.HBM) if i in hbm_in else o for i, o in enumerate(operands)]
    return kernel(*operands)


def shards(queries, passages, positive):
    count, width = queries.shape
    rows = passages.shape[0]
    scale = 3.0 / math.sqrt(width)
    nz, nx = lax.axis_size("z"), lax.axis_size("x")
    ny = lax.axis_size("yh") * 2
    x, c = lax.axis_index("x"), lax.axis_index("c")
    y = lax.axis_index("yh") * 2 + lax.axis_index("yl")
    n = nz * rows
    flops = 2 * n * width * count

    def base_of(yy, cc):
        yy = (yy + ny) & (ny - 1)
        return ((((yy >> 1) * nx + x) * nz * 2 + (yy & 1)) * 2 + cc) * rows

    base = jnp.stack(
        [base_of(y, c), base_of(y, 1 - c), base_of(y + 1 - 2 * c, c), base_of(y - 1 + 2 * c, 1 - c), y & 1]
    )
    pos = positive.reshape(1, count)

    theirs = to_sides(queries, ny)
    pos_theirs = to_sides(pos, ny)
    (copies,) = call(
        copy_kernel,
        [((nz, rows, width), BF16)],
        (passages,),
        [((rows, width), BF16), pltpu.SemaphoreType.DMA((nz + 1,))],
        hbm_in=(0,),
        hbm_out=(0,),
    )
    column = lax.all_to_all(copies, "z", split_axis=0, concat_axis=0, tiled=True)
    column, theirs, pos_theirs = lax.optimization_barrier((column, theirs, pos_theirs))
    column = column.reshape(n, width)
    side = to_sides(column, ny)
    column2 = swapped(column)
    members = ny * nx
    st1, weights, stats = call(
        functools.partial(stat_kernel, scale, rows),
        [((8, count), F32), ((2 * n, count), BF16), ((members, 1, 2 * count), F32)],
        (base, column, column2, queries, pos, theirs, pos_theirs),
        [((2 * n, count), F32), ((2 * n, count), BF16), pltpu.SemaphoreType.DMA],
        4 * flops,
        hbm_out=(1,),
    )
    every = lax.all_to_all(stats, ("yl", *OUTER), split_axis=0, concat_axis=0, tiled=True)
    side2 = swapped(side)
    queries, side = call(
        load_kernel,
        [(queries.shape, BF16), ((n, width), BF16)],
        (queries, side),
        [pltpu.SemaphoreType.DMA((2,))],
        vmem=4,
        hbm_in=(0, 1),
    )
    st, m, ch = call(
        functools.partial(mix_kernel, scale, rows),
        [((8, count), F32), ((width, count), F32), ((width, count), BF16)],
        (base, column, column2, weights, side, side2, queries, pos, st1),
        [
            ((2 * n, count), F32),
            ((2 * n, count), BF16),
            ((n, width), BF16),
            ((n, width), BF16),
            ((2 * n, count), BF16),
            pltpu.SemaphoreType.DMA((3,)),
        ],
        10 * flops,
        vmem=24,
        hbm_in=(1, 2, 3),
    )
    out, loss = call(
        functools.partial(scale_kernel, scale), [((width, count), BF16), ((1, count), F32)], (every, st, m, ch)
    )
    n_outer = members // 2
    out = out.reshape(n_outer, width // n_outer, count)
    got = lax.all_to_all(out, OUTER, split_axis=0, concat_axis=0, tiled=True)
    (grad,) = call(functools.partial(final_kernel, scale), [((width // n_outer, count), BF16)], (got,))
    return grad.T, loss.reshape(count)


def solution(mesh):
    devices = mesh.devices
    torus = Mesh(devices.reshape(4, 4, 8, 2, 2), ("yh", "x", "z", "yl", "c"))
    in_specs = (P(INNER, None), P((*OUTER, *INNER), None), P(INNER))
    out_specs = (P(INNER, OUTER), P(INNER))
    return jax.shard_map(shards, mesh=torus, in_specs=in_specs, out_specs=out_specs, check_vma=False)
```

```python
import functools
import math

import jax
import jax.numpy as jnp
from jax import lax
from jax.experimental import pallas as pl
from jax.experimental.pallas import tpu as pltpu
from jax.sharding import Mesh
from jax.sharding import PartitionSpec as P


INNER = ("z", "yl", "c")
OUTER = ("yh", "x")
LANE = ("yh", "yl", "c")
F32, BF16 = jnp.float32, jnp.bfloat16
LOG2E = math.log2(math.e)
VMEM = pl.BlockSpec(memory_space=pltpu.VMEM)
SMEM = pl.BlockSpec(memory_space=pltpu.SMEM)
HBM = pl.BlockSpec(memory_space=pltpu.HBM)


def swapped(x):
    return lax.ppermute(x, "c", [(0, 1), (1, 0)])


def to_sides(x, ny):
    perm = []
    for y in range(ny):
        perm.append((2 * y, 2 * ((y - 1) % ny)))
        perm.append((2 * y + 1, 2 * ((y + 1) % ny) + 1))
    return lax.ppermute(x, LANE, perm)


def dot(a, b, dims):
    return lax.dot_general(a, b, (dims, ((), ())), preferred_element_type=F32)


def hits_of(pos_ref, base, count, rows):
    j = lax.broadcasted_iota(jnp.int32, (count, 1), 0)
    return (j // rows) * (4 * rows) + j % rows == pos_ref[...] - base


def statistics(p_refs, bases, q_ref, pos_ref, s_ref, rows):
    q = q_ref[...]
    top = ps = None
    for i, p_ref in enumerate(p_refs):
        n = p_ref.shape[0]
        s = dot(p_ref[...], q, ((1,), (1,)))
        s_ref[i * n : (i + 1) * n, :] = s
        hit = hits_of(pos_ref, bases[i], n, rows)
        t = jnp.max(s, axis=0, keepdims=True)
        u = jnp.sum(jnp.where(hit, s, 0.0), axis=0, keepdims=True)
        top = t if top is None else jnp.maximum(top, t)
        ps = u if ps is None else ps + u
    return top, ps


def products(p_refs, bases, w_ref, pos_ref, rows):
    mix = chosen = 0.0
    for i, p_ref in enumerate(p_refs):
        n = p_ref.shape[0]
        p = p_ref[...]
        hit = hits_of(pos_ref, bases[i], n, rows).astype(F32).astype(BF16)
        mix += dot(p, w_ref[i * n : (i + 1) * n, :], ((0,), (0,)))
        chosen += dot(p, hit, ((0,), (0,)))
    return mix, chosen


def stat_kernel(scale, rows, base_ref, a_ref, b_ref, q_ref, pos_ref, qf_ref, posf_ref, st_ref, w_hbm, out_ref, s_ref, w_ref, sem):
    bases = (base_ref[0], base_ref[1])
    pieces = []
    for qq, pp in ((q_ref, pos_ref), (qf_ref, posf_ref)):
        top, ps = statistics((a_ref, b_ref), bases, qq, pp, s_ref, rows)
        e = jnp.exp2((s_ref[...] - top) * (scale * LOG2E))
        total = jnp.sum(e, axis=0, keepdims=True)
        if not pieces:
            w_ref[...] = e.astype(BF16)
            copy = pltpu.make_async_copy(w_ref, w_hbm, sem)
            copy.start()
            st_ref[0:1, :] = top
        pieces.append(jnp.concatenate([top * scale + jnp.log(total), ps * scale], axis=1))
    own, theirs = pieces
    lower = base_ref[4] == 0
    half = out_ref.shape[0] // 2
    shape = (half, *own.shape)
    out_ref[:half] = jnp.broadcast_to(jnp.where(lower, own, theirs)[None], shape)
    out_ref[half:] = jnp.broadcast_to(jnp.where(lower, theirs, own)[None], shape)
    copy.wait()


def load_kernel(*refs):
    count = (len(refs) - 1) // 2
    copies = [pltpu.make_async_copy(refs[i], refs[count + i], refs[-1].at[i]) for i in range(count)]
    for copy in copies:
        copy.start()
    for copy in copies:
        copy.wait()


def mix_kernel(scale, rows, base_ref, a_hbm, b_hbm, wo_hbm, side_ref, side2_ref, q_ref, pos_ref, st0_ref, st_ref, m_ref, c_ref, s_ref, w_ref, a_ref, b_ref, wo_ref, sems):
    pairs = ((a_hbm, a_ref), (b_hbm, b_ref), (wo_hbm, wo_ref))
    copies = [pltpu.make_async_copy(src, dst, sems.at[i]) for i, (src, dst) in enumerate(pairs)]
    for copy in copies:
        copy.start()
    q = q_ref[...]
    n = side2_ref.shape[0]
    s_ref[:n, :] = dot(side2_ref[...], q, ((1,), (1,)))
    s_ref[n:, :] = dot(side_ref[...], q, ((1,), (1,)))
    top0 = st0_ref[0:1, :]
    top = jnp.maximum(jnp.max(s_ref[...], axis=0, keepdims=True), top0)
    w_ref[...] = jnp.exp2((s_ref[...] - top) * (scale * LOG2E)).astype(BF16)
    st_ref[0:1, :] = top
    mix, chosen = products((side2_ref, side_ref), (base_ref[3], base_ref[2]), w_ref, pos_ref, rows)
    m_ref[...] = mix
    for copy in copies:
        copy.wait()
    mix, more = products((a_ref, b_ref), (base_ref[0], base_ref[1]), wo_ref, pos_ref, rows)
    m_ref[...] += mix * jnp.exp2((top0 - top) * (scale * LOG2E))
    c_ref[...] = (chosen + more).astype(BF16)


def scale_kernel(scale, every_ref, st_ref, m_ref, c_ref, out_ref, loss_ref):
    count = m_ref.shape[1]
    lse = every_ref[:, 0, :count]
    most = jnp.max(lse, axis=0, keepdims=True)
    whole = most + jnp.log(jnp.sum(jnp.exp(lse - most), axis=0, keepdims=True))
    ps = jnp.sum(every_ref[:, 0, count:], axis=0, keepdims=True)
    g = jnp.exp(st_ref[0:1, :] * scale - whole)
    out = (m_ref[...] * g - c_ref[...].astype(F32)).astype(BF16)
    nx, width, _ = out_ref.shape
    piece = width // 4
    for i in range(nx):
        for j in range(4):
            at = (j * nx + i) * piece
            out_ref[i, j * piece : (j + 1) * piece, :] = out[at : at + piece]
    loss_ref[...] = whole - ps


def copy_kernel(x_hbm, out_hbm, x_ref, sems):
    n = out_hbm.shape[0]
    first = pltpu.make_async_copy(x_hbm, x_ref, sems.at[n])
    first.start()
    first.wait()
    copies = [pltpu.make_async_copy(x_ref, out_hbm.at[i], sems.at[i]) for i in range(n)]
    for copy in copies:
        copy.start()
    for copy in copies:
        copy.wait()


def sum_kernel(scale, got_ref, out_ref):
    total = got_ref[0].astype(F32)
    for i in range(1, got_ref.shape[0]):
        total += got_ref[i].astype(F32)
    out_ref[...] = (scale * total).astype(BF16)


def call(body, out, operands, scratch=(), flops=0, vmem=12, hbm_in=(), hbm_out=()):
    def spec(i, o):
        if i in hbm_in:
            return HBM
        return SMEM if o.dtype == jnp.int32 and o.ndim == 1 else VMEM

    kernel = pl.pallas_call(
        body,
        in_specs=[spec(i, o) for i, o in enumerate(operands)],
        out_specs=[HBM if i in hbm_out else VMEM for i in range(len(out))],
        out_shape=[pltpu.HBM(s, d) if i in hbm_out else jax.ShapeDtypeStruct(s, d) for i, (s, d) in enumerate(out)],
        scratch_shapes=[s if not isinstance(s, tuple) else pltpu.VMEM(*s) for s in scratch],
        cost_estimate=pl.CostEstimate(flops=flops, bytes_accessed=4 << 20, transcendentals=0),
        compiler_params=pltpu.CompilerParams(vmem_limit_bytes=vmem << 20),
    )
    operands = [pltpu.with_memory_space_constraint(o, pltpu.HBM) if i in hbm_in else o for i, o in enumerate(operands)]
    return kernel(*operands)


def shards(queries, passages, positive):
    count, width = queries.shape
    rows = passages.shape[0]
    scale = 3.0 / math.sqrt(width)
    nz, nx = lax.axis_size("z"), lax.axis_size("x")
    ny = lax.axis_size("yh") * 2
    x, c = lax.axis_index("x"), lax.axis_index("c")
    y = lax.axis_index("yh") * 2 + lax.axis_index("yl")
    n = nz * rows
    flops = 2 * n * width * count

    def base_of(yy, cc):
        yy = (yy + ny) & (ny - 1)
        return ((((yy >> 1) * nx + x) * nz * 2 + (yy & 1)) * 2 + cc) * rows

    base = jnp.stack(
        [base_of(y, c), base_of(y, 1 - c), base_of(y + 1 - 2 * c, c), base_of(y - 1 + 2 * c, 1 - c), y & 1]
    )
    pos = positive.reshape(1, count)

    theirs = to_sides(queries, ny)
    pos_theirs = to_sides(pos, ny)
    (copies,) = call(
        copy_kernel,
        [((nz, rows, width), BF16)],
        (passages,),
        [((rows, width), BF16), pltpu.SemaphoreType.DMA((nz + 1,))],
        hbm_in=(0,),
        hbm_out=(0,),
    )
    column = lax.all_to_all(copies, "z", split_axis=0, concat_axis=0, tiled=True)
    column, theirs, pos_theirs = lax.optimization_barrier((column, theirs, pos_theirs))
    column = column.reshape(n, width)
    side = to_sides(column, ny)
    column2 = swapped(column)
    members = ny * nx
    st1, weights, stats = call(
        functools.partial(stat_kernel, scale, rows),
        [((8, count), F32), ((2 * n, count), BF16), ((members, 1, 2 * count), F32)],
        (base, column, column2, queries, pos, theirs, pos_theirs),
        [((2 * n, count), F32), ((2 * n, count), BF16), pltpu.SemaphoreType.DMA],
        4 * flops,
        hbm_out=(1,),
    )
    every = lax.all_to_all(stats, ("yl", *OUTER), split_axis=0, concat_axis=0, tiled=True)
    side2 = swapped(side)
    queries, side = call(
        load_kernel,
        [(queries.shape, BF16), ((n, width), BF16)],
        (queries, side),
        [pltpu.SemaphoreType.DMA((2,))],
        vmem=4,
        hbm_in=(0, 1),
    )
    st, m, ch = call(
        functools.partial(mix_kernel, scale, rows),
        [((8, count), F32), ((width, count), F32), ((width, count), BF16)],
        (base, column, column2, weights, side, side2, queries, pos, st1),
        [
            ((2 * n, count), F32),
            ((2 * n, count), BF16),
            ((n, width), BF16),
            ((n, width), BF16),
            ((2 * n, count), BF16),
            pltpu.SemaphoreType.DMA((3,)),
        ],
        10 * flops,
        vmem=24,
        hbm_in=(1, 2, 3),
    )
    out, loss = call(
        functools.partial(scale_kernel, scale),
        [((nx, width // nx, count), BF16), ((1, count), F32)],
        (every, st, m, ch),
    )
    got = lax.all_to_all(out, "x", split_axis=0, concat_axis=0, tiled=True)
    (out,) = call(functools.partial(sum_kernel, 1.0), [((width // nx, count), BF16)], (got,))
    nyh = ny // 2
    piece = width // nx // nyh
    out = out.reshape(nyh, piece, count)
    got = lax.all_to_all(out, "yh", split_axis=0, concat_axis=0, tiled=True)
    (grad,) = call(functools.partial(sum_kernel, scale), [((piece, count), BF16)], (got,))
    return grad.T, loss.reshape(count)


def solution(mesh):
    devices = mesh.devices
    torus = Mesh(devices.reshape(4, 4, 8, 2, 2), ("yh", "x", "z", "yl", "c"))
    in_specs = (P(INNER, None), P((*OUTER, *INNER), None), P(INNER))
    out_specs = (P(INNER, OUTER), P(INNER))
    return jax.shard_map(shards, mesh=torus, in_specs=in_specs, out_specs=out_specs, check_vma=False)
```

```python
import functools
import math

import jax
import jax.numpy as jnp
from jax import lax
from jax.experimental import pallas as pl
from jax.experimental.pallas import tpu as pltpu
from jax.sharding import Mesh
from jax.sharding import PartitionSpec as P


INNER = ("z", "yl", "c")
OUTER = ("yh", "x")
LANE = ("yh", "yl", "c")
F32, BF16 = jnp.float32, jnp.bfloat16
LOG2E = math.log2(math.e)
VMEM = pl.BlockSpec(memory_space=pltpu.VMEM)
SMEM = pl.BlockSpec(memory_space=pltpu.SMEM)
HBM = pl.BlockSpec(memory_space=pltpu.HBM)


def swapped(x):
    return lax.ppermute(x, "c", [(0, 1), (1, 0)])


def to_sides(x, ny):
    perm = []
    for y in range(ny):
        perm.append((2 * y, 2 * ((y - 1) % ny)))
        perm.append((2 * y + 1, 2 * ((y + 1) % ny) + 1))
    return lax.ppermute(x, LANE, perm)


def dot(a, b, dims):
    return lax.dot_general(a, b, (dims, ((), ())), preferred_element_type=F32)


def hits_of(pos_ref, base, count, rows):
    j = lax.broadcasted_iota(jnp.int32, (count, 1), 0)
    return (j // rows) * (4 * rows) + j % rows == pos_ref[...] - base


def products(p_refs, bases, w_ref, pos_ref, rows):
    mix = chosen = 0.0
    for i, p_ref in enumerate(p_refs):
        n = p_ref.shape[0]
        p = p_ref[...]
        hit = hits_of(pos_ref, bases[i], n, rows).astype(F32).astype(BF16)
        mix += dot(p, w_ref[i * n : (i + 1) * n, :], ((0,), (0,)))
        chosen += dot(p, hit, ((0,), (0,)))
    return mix, chosen


def half_statistics(scale, rows, base, p_ref, q_ref, pos_ref, s_ref):
    s_ref[...] = dot(p_ref[...], q_ref[...], ((1,), (1,)))
    hit = hits_of(pos_ref, base, p_ref.shape[0], rows)
    top = jnp.max(s_ref[...], axis=0, keepdims=True)
    ps = jnp.sum(jnp.where(hit, s_ref[...], 0.0), axis=0, keepdims=True)
    e = jnp.exp2((s_ref[...] - top) * (scale * LOG2E))
    lse = top * scale + jnp.log(jnp.sum(e, axis=0, keepdims=True))
    return top, e, lse, ps * scale


def stata_kernel(scale, rows, base_ref, a_ref, q_ref, pos_ref, qf_ref, posf_ref, st_ref, w_hbm, s_ref, w_ref, sem):
    top, e, lse, ps = half_statistics(scale, rows, base_ref[0], a_ref, q_ref, pos_ref, s_ref)
    w_ref[...] = e.astype(BF16)
    copy = pltpu.make_async_copy(w_ref, w_hbm, sem)
    copy.start()
    _, _, lse2, ps2 = half_statistics(scale, rows, base_ref[0], a_ref, qf_ref, posf_ref, s_ref)
    for i, row in enumerate((top, lse, ps, lse2, ps2)):
        st_ref[i : i + 1, :] = row
    copy.wait()


def statb_kernel(scale, rows, base_ref, b_ref, q_ref, pos_ref, qf_ref, posf_ref, st0_ref, st_ref, w_hbm, out_ref, s_ref, w_ref, sem):
    pieces = []
    for i, (qq, pp) in enumerate(((q_ref, pos_ref), (qf_ref, posf_ref))):
        top, e, lse, ps = half_statistics(scale, rows, base_ref[1], b_ref, qq, pp, s_ref)
        if i == 0:
            w_ref[...] = e.astype(BF16)
            copy = pltpu.make_async_copy(w_ref, w_hbm, sem)
            copy.start()
            st_ref[0:1, :] = st0_ref[0:1, :]
            st_ref[1:2, :] = top
        lse0, ps0 = st0_ref[2 * i + 1 : 2 * i + 2, :], st0_ref[2 * i + 2 : 2 * i + 3, :]
        most = jnp.maximum(lse, lse0)
        lse = most + jnp.log(jnp.exp(lse - most) + jnp.exp(lse0 - most))
        pieces.append(jnp.concatenate([lse, ps + ps0], axis=1))
    own, theirs = pieces
    lower = base_ref[4] == 0
    half = out_ref.shape[0] // 2
    shape = (half, *own.shape)
    out_ref[:half] = jnp.broadcast_to(jnp.where(lower, own, theirs)[None], shape)
    out_ref[half:] = jnp.broadcast_to(jnp.where(lower, theirs, own)[None], shape)
    copy.wait()


def side_kernel(q_hbm, side_hbm, q_ref, side_ref, s_ref, sems):
    pairs = ((q_hbm, q_ref), (side_hbm, side_ref))
    copies = [pltpu.make_async_copy(src, dst, sems.at[i]) for i, (src, dst) in enumerate(pairs)]
    for copy in copies:
        copy.start()
    for copy in copies:
        copy.wait()
    s_ref[...] = dot(side_ref[...], q_ref[...], ((1,), (1,)))


def mix_kernel(scale, rows, base_ref, a_hbm, b_hbm, wa_hbm, wb_hbm, side_ref, ss_ref, side2_ref, q_ref, pos_ref, st0_ref, st_ref, m_ref, c_ref, s_ref, w_ref, a_ref, b_ref, wa_ref, wb_ref, sems):
    pairs = ((a_hbm, a_ref), (wa_hbm, wa_ref), (b_hbm, b_ref), (wb_hbm, wb_ref))
    copies = [pltpu.make_async_copy(src, dst, sems.at[i]) for i, (src, dst) in enumerate(pairs)]
    for copy in copies:
        copy.start()
    n = side2_ref.shape[0]
    k = scale * LOG2E
    s_ref[...] = dot(side2_ref[...], q_ref[...], ((1,), (1,)))
    tops = [st0_ref[0:1, :], st0_ref[1:2, :]]
    top = jnp.maximum(jnp.max(s_ref[...], axis=0, keepdims=True), jnp.max(ss_ref[...], axis=0, keepdims=True))
    top = jnp.maximum(top, jnp.maximum(*tops))
    st_ref[0:1, :] = top
    w_ref[:n, :] = jnp.exp2((s_ref[...] - top) * k).astype(BF16)
    w_ref[n:, :] = jnp.exp2((ss_ref[...] - top) * k).astype(BF16)
    mix, chosen = products((side2_ref, side_ref), (base_ref[3], base_ref[2]), w_ref, pos_ref, rows)
    m_ref[...] = mix
    for copy in copies:
        copy.wait()
    for p_ref, wo_ref, base, top0 in zip((a_ref, b_ref), (wa_ref, wb_ref), (base_ref[0], base_ref[1]), tops):
        mix, more = products((p_ref,), (base,), wo_ref, pos_ref, rows)
        m_ref[...] += mix * jnp.exp2((top0 - top) * k)
        chosen += more
    c_ref[...] = chosen.astype(BF16)


def scale_kernel(scale, every_ref, st_ref, m_ref, c_ref, out_ref, loss_ref):
    count = m_ref.shape[1]
    lse = every_ref[:, 0, :count]
    most = jnp.max(lse, axis=0, keepdims=True)
    whole = most + jnp.log(jnp.sum(jnp.exp(lse - most), axis=0, keepdims=True))
    ps = jnp.sum(every_ref[:, 0, count:], axis=0, keepdims=True)
    g = jnp.exp(st_ref[0:1, :] * scale - whole)
    out = (m_ref[...] * g - c_ref[...].astype(F32)).astype(BF16)
    nx, width, _ = out_ref.shape
    piece = width // 4
    for i in range(nx):
        for j in range(4):
            at = (j * nx + i) * piece
            out_ref[i, j * piece : (j + 1) * piece, :] = out[at : at + piece]
    loss_ref[...] = whole - ps


def copy_kernel(x_hbm, out_hbm, x_ref, sems):
    n = out_hbm.shape[0]
    first = pltpu.make_async_copy(x_hbm, x_ref, sems.at[n])
    first.start()
    first.wait()
    copies = [pltpu.make_async_copy(x_ref, out_hbm.at[i], sems.at[i]) for i in range(n)]
    for copy in copies:
        copy.start()
    for copy in copies:
        copy.wait()


def sum_kernel(scale, got_ref, out_ref):
    total = got_ref[0].astype(F32)
    for i in range(1, got_ref.shape[0]):
        total += got_ref[i].astype(F32)
    out_ref[...] = (scale * total).astype(BF16)


def call(body, out, operands, scratch=(), flops=0, vmem=12, hbm_in=(), hbm_out=()):
    def spec(i, o):
        if i in hbm_in:
            return HBM
        return SMEM if o.dtype == jnp.int32 and o.ndim == 1 else VMEM

    kernel = pl.pallas_call(
        body,
        in_specs=[spec(i, o) for i, o in enumerate(operands)],
        out_specs=[HBM if i in hbm_out else VMEM for i in range(len(out))],
        out_shape=[pltpu.HBM(s, d) if i in hbm_out else jax.ShapeDtypeStruct(s, d) for i, (s, d) in enumerate(out)],
        scratch_shapes=[s if not isinstance(s, tuple) else pltpu.VMEM(*s) for s in scratch],
        cost_estimate=pl.CostEstimate(flops=flops, bytes_accessed=4 << 20, transcendentals=0),
        compiler_params=pltpu.CompilerParams(vmem_limit_bytes=vmem << 20),
    )
    operands = [pltpu.with_memory_space_constraint(o, pltpu.HBM) if i in hbm_in else o for i, o in enumerate(operands)]
    return kernel(*operands)


def shards(queries, passages, positive):
    count, width = queries.shape
    rows = passages.shape[0]
    scale = 3.0 / math.sqrt(width)
    nz, nx = lax.axis_size("z"), lax.axis_size("x")
    ny = lax.axis_size("yh") * 2
    x, c = lax.axis_index("x"), lax.axis_index("c")
    y = lax.axis_index("yh") * 2 + lax.axis_index("yl")
    n = nz * rows
    flops = 2 * n * width * count

    def base_of(yy, cc):
        yy = (yy + ny) & (ny - 1)
        return ((((yy >> 1) * nx + x) * nz * 2 + (yy & 1)) * 2 + cc) * rows

    base = jnp.stack(
        [base_of(y, c), base_of(y, 1 - c), base_of(y + 1 - 2 * c, c), base_of(y - 1 + 2 * c, 1 - c), y & 1]
    )
    pos = positive.reshape(1, count)

    theirs = to_sides(queries, ny)
    pos_theirs = to_sides(pos, ny)
    (copies,) = call(
        copy_kernel,
        [((nz, rows, width), BF16)],
        (passages,),
        [((rows, width), BF16), pltpu.SemaphoreType.DMA((nz + 1,))],
        hbm_in=(0,),
        hbm_out=(0,),
    )
    column = lax.all_to_all(copies, "z", split_axis=0, concat_axis=0, tiled=True)
    column, theirs, pos_theirs = lax.optimization_barrier((column, theirs, pos_theirs))
    column = column.reshape(n, width)
    side = to_sides(column, ny)
    column2 = swapped(column)
    members = ny * nx
    scratch = [((n, count), F32), ((n, count), BF16), pltpu.SemaphoreType.DMA]
    st0, wa = call(
        functools.partial(stata_kernel, scale, rows),
        [((8, count), F32), ((n, count), BF16)],
        (base, column, queries, pos, theirs, pos_theirs),
        scratch,
        2 * flops,
        hbm_out=(1,),
    )
    st1, wb, stats = call(
        functools.partial(statb_kernel, scale, rows),
        [((8, count), F32), ((n, count), BF16), ((members, 1, 2 * count), F32)],
        (base, column2, queries, pos, theirs, pos_theirs, st0),
        scratch,
        2 * flops,
        hbm_out=(1,),
    )
    every = lax.all_to_all(stats, ("yl", *OUTER), split_axis=0, concat_axis=0, tiled=True)
    side2 = swapped(side)
    queries, side, scores = call(
        side_kernel,
        [(queries.shape, BF16), ((n, width), BF16), ((n, count), F32)],
        (queries, side),
        [pltpu.SemaphoreType.DMA((2,))],
        flops,
        vmem=8,
        hbm_in=(0, 1),
    )
    st, m, ch = call(
        functools.partial(mix_kernel, scale, rows),
        [((8, count), F32), ((width, count), F32), ((width, count), BF16)],
        (base, column, column2, wa, wb, side, scores, side2, queries, pos, st1),
        [
            ((n, count), F32),
            ((2 * n, count), BF16),
            ((n, width), BF16),
            ((n, width), BF16),
            ((n, count), BF16),
            ((n, count), BF16),
            pltpu.SemaphoreType.DMA((4,)),
        ],
        10 * flops,
        vmem=24,
        hbm_in=(1, 2, 3, 4),
    )
    out, loss = call(
        functools.partial(scale_kernel, scale),
        [((nx, width // nx, count), BF16), ((1, count), F32)],
        (every, st, m, ch),
    )
    got = lax.all_to_all(out, "x", split_axis=0, concat_axis=0, tiled=True)
    (out,) = call(functools.partial(sum_kernel, 1.0), [((width // nx, count), BF16)], (got,))
    nyh = ny // 2
    piece = width // nx // nyh
    out = out.reshape(nyh, piece, count)
    got = lax.all_to_all(out, "yh", split_axis=0, concat_axis=0, tiled=True)
    (grad,) = call(functools.partial(sum_kernel, scale), [((piece, count), BF16)], (got,))
    return grad.T, loss.reshape(count)


def solution(mesh):
    devices = mesh.devices
    torus = Mesh(devices.reshape(4, 4, 8, 2, 2), ("yh", "x", "z", "yl", "c"))
    in_specs = (P(INNER, None), P((*OUTER, *INNER), None), P(INNER))
    out_specs = (P(INNER, OUTER), P(INNER))
    return jax.shard_map(shards, mesh=torus, in_specs=in_specs, out_specs=out_specs, check_vma=False)
```

```python
import functools
import math

import jax
import jax.numpy as jnp
from jax import lax
from jax.experimental import pallas as pl
from jax.experimental.pallas import tpu as pltpu
from jax.sharding import Mesh
from jax.sharding import PartitionSpec as P


INNER = ("z", "yl", "c")
OUTER = ("yh", "x")
LANE = ("yh", "yl", "c")
F32, BF16 = jnp.float32, jnp.bfloat16
LOG2E = math.log2(math.e)
VMEM = pl.BlockSpec(memory_space=pltpu.VMEM)
SMEM = pl.BlockSpec(memory_space=pltpu.SMEM)
HBM = pl.BlockSpec(memory_space=pltpu.HBM)


def swapped(x):
    return lax.ppermute(x, "c", [(0, 1), (1, 0)])


def to_sides(x, ny):
    perm = []
    for y in range(ny):
        perm.append((2 * y, 2 * ((y - 1) % ny)))
        perm.append((2 * y + 1, 2 * ((y + 1) % ny) + 1))
    return lax.ppermute(x, LANE, perm)


def dot(a, b, dims):
    return lax.dot_general(a, b, (dims, ((), ())), preferred_element_type=F32)


def hits_of(pos_ref, base, count, rows):
    j = lax.broadcasted_iota(jnp.int32, (count, 1), 0)
    return (j // rows) * (4 * rows) + j % rows == pos_ref[...] - base


def statistics(p_refs, bases, q_ref, pos_ref, s_ref, rows):
    q = q_ref[...]
    top = ps = None
    for i, p_ref in enumerate(p_refs):
        n = p_ref.shape[0]
        s = dot(p_ref[...], q, ((1,), (1,)))
        s_ref[i * n : (i + 1) * n, :] = s
        hit = hits_of(pos_ref, bases[i], n, rows)
        t = jnp.max(s, axis=0, keepdims=True)
        u = jnp.sum(jnp.where(hit, s, 0.0), axis=0, keepdims=True)
        top = t if top is None else jnp.maximum(top, t)
        ps = u if ps is None else ps + u
    return top, ps


def products(p_refs, bases, w_ref, pos_ref, rows):
    mix = chosen = 0.0
    for i, p_ref in enumerate(p_refs):
        n = p_ref.shape[0]
        p = p_ref[...]
        hit = hits_of(pos_ref, bases[i], n, rows).astype(F32).astype(BF16)
        mix += dot(p, w_ref[i * n : (i + 1) * n, :], ((0,), (0,)))
        chosen += dot(p, hit, ((0,), (0,)))
    return mix, chosen


def stat_kernel(scale, rows, base_ref, a_ref, b_ref, q_ref, pos_ref, qf_ref, posf_ref, st_ref, w_hbm, out_ref, s_ref, w_ref, sem):
    bases = (base_ref[0], base_ref[1])
    pieces = []
    for qq, pp in ((q_ref, pos_ref), (qf_ref, posf_ref)):
        top, ps = statistics((a_ref, b_ref), bases, qq, pp, s_ref, rows)
        e = jnp.exp2((s_ref[...] - top) * (scale * LOG2E))
        total = jnp.sum(e, axis=0, keepdims=True)
        if not pieces:
            w_ref[...] = e.astype(BF16)
            copy = pltpu.make_async_copy(w_ref, w_hbm, sem)
            copy.start()
            st_ref[0:1, :] = top
        pieces.append(jnp.concatenate([top * scale + jnp.log(total), ps * scale], axis=1))
    own, theirs = pieces
    lower = base_ref[4] == 0
    half = out_ref.shape[0] // 2
    shape = (half, *own.shape)
    out_ref[:half] = jnp.broadcast_to(jnp.where(lower, own, theirs)[None], shape)
    out_ref[half:] = jnp.broadcast_to(jnp.where(lower, theirs, own)[None], shape)
    copy.wait()


def side_kernel(q_hbm, side_hbm, q_ref, side_ref, s_ref, sems):
    pairs = ((q_hbm, q_ref), (side_hbm, side_ref))
    copies = [pltpu.make_async_copy(src, dst, sems.at[i]) for i, (src, dst) in enumerate(pairs)]
    for copy in copies:
        copy.start()
    for copy in copies:
        copy.wait()
    s_ref[...] = dot(side_ref[...], q_ref[...], ((1,), (1,)))


def mix_kernel(scale, rows, base_ref, a_hbm, b_hbm, wo_hbm, side_ref, ss_ref, side2_ref, q_ref, pos_ref, st0_ref, st_ref, m_ref, c_ref, s_ref, w_ref, a_ref, b_ref, wo_ref, sems):
    pairs = ((a_hbm, a_ref), (b_hbm, b_ref), (wo_hbm, wo_ref))
    copies = [pltpu.make_async_copy(src, dst, sems.at[i]) for i, (src, dst) in enumerate(pairs)]
    for copy in copies:
        copy.start()
    n = side2_ref.shape[0]
    k = scale * LOG2E
    s_ref[...] = dot(side2_ref[...], q_ref[...], ((1,), (1,)))
    top0 = st0_ref[0:1, :]
    top = jnp.maximum(jnp.max(s_ref[...], axis=0, keepdims=True), jnp.max(ss_ref[...], axis=0, keepdims=True))
    top = jnp.maximum(top, top0)
    st_ref[0:1, :] = top
    w_ref[:n, :] = jnp.exp2((s_ref[...] - top) * k).astype(BF16)
    w_ref[n:, :] = jnp.exp2((ss_ref[...] - top) * k).astype(BF16)
    mix, chosen = products((side2_ref, side_ref), (base_ref[3], base_ref[2]), w_ref, pos_ref, rows)
    m_ref[...] = mix
    for copy in copies:
        copy.wait()
    mix, more = products((a_ref, b_ref), (base_ref[0], base_ref[1]), wo_ref, pos_ref, rows)
    m_ref[...] += mix * jnp.exp2((top0 - top) * k)
    c_ref[...] = (chosen + more).astype(BF16)


def scale_kernel(scale, every_ref, st_ref, m_ref, c_ref, out_ref, loss_ref):
    count = m_ref.shape[1]
    lse = every_ref[:, 0, :count]
    most = jnp.max(lse, axis=0, keepdims=True)
    whole = most + jnp.log(jnp.sum(jnp.exp(lse - most), axis=0, keepdims=True))
    ps = jnp.sum(every_ref[:, 0, count:], axis=0, keepdims=True)
    g = jnp.exp(st_ref[0:1, :] * scale - whole)
    out = (m_ref[...] * g - c_ref[...].astype(F32)).astype(BF16)
    nx, width, _ = out_ref.shape
    piece = width // 4
    for i in range(nx):
        for j in range(4):
            at = (j * nx + i) * piece
            out_ref[i, j * piece : (j + 1) * piece, :] = out[at : at + piece]
    loss_ref[...] = whole - ps


def copy_kernel(x_hbm, out_hbm, x_ref, sems):
    n = out_hbm.shape[0]
    first = pltpu.make_async_copy(x_hbm, x_ref, sems.at[n])
    first.start()
    first.wait()
    copies = [pltpu.make_async_copy(x_ref, out_hbm.at[i], sems.at[i]) for i in range(n)]
    for copy in copies:
        copy.start()
    for copy in copies:
        copy.wait()


def sum_kernel(scale, got_ref, out_ref):
    total = got_ref[0].astype(F32)
    for i in range(1, got_ref.shape[0]):
        total += got_ref[i].astype(F32)
    out_ref[...] = (scale * total).astype(BF16)


def call(body, out, operands, scratch=(), flops=0, vmem=12, hbm_in=(), hbm_out=()):
    def spec(i, o):
        if i in hbm_in:
            return HBM
        return SMEM if o.dtype == jnp.int32 and o.ndim == 1 else VMEM

    kernel = pl.pallas_call(
        body,
        in_specs=[spec(i, o) for i, o in enumerate(operands)],
        out_specs=[HBM if i in hbm_out else VMEM for i in range(len(out))],
        out_shape=[pltpu.HBM(s, d) if i in hbm_out else jax.ShapeDtypeStruct(s, d) for i, (s, d) in enumerate(out)],
        scratch_shapes=[s if not isinstance(s, tuple) else pltpu.VMEM(*s) for s in scratch],
        cost_estimate=pl.CostEstimate(flops=flops, bytes_accessed=4 << 20, transcendentals=0),
        compiler_params=pltpu.CompilerParams(vmem_limit_bytes=vmem << 20),
    )
    operands = [pltpu.with_memory_space_constraint(o, pltpu.HBM) if i in hbm_in else o for i, o in enumerate(operands)]
    return kernel(*operands)


def shards(queries, passages, positive):
    count, width = queries.shape
    rows = passages.shape[0]
    scale = 3.0 / math.sqrt(width)
    nz, nx = lax.axis_size("z"), lax.axis_size("x")
    ny = lax.axis_size("yh") * 2
    x, c = lax.axis_index("x"), lax.axis_index("c")
    y = lax.axis_index("yh") * 2 + lax.axis_index("yl")
    n = nz * rows
    flops = 2 * n * width * count

    def base_of(yy, cc):
        yy = (yy + ny) & (ny - 1)
        return ((((yy >> 1) * nx + x) * nz * 2 + (yy & 1)) * 2 + cc) * rows

    base = jnp.stack(
        [base_of(y, c), base_of(y, 1 - c), base_of(y + 1 - 2 * c, c), base_of(y - 1 + 2 * c, 1 - c), y & 1]
    )
    pos = positive.reshape(1, count)

    theirs = to_sides(queries, ny)
    pos_theirs = to_sides(pos, ny)
    (copies,) = call(
        copy_kernel,
        [((nz, rows, width), BF16)],
        (passages,),
        [((rows, width), BF16), pltpu.SemaphoreType.DMA((nz + 1,))],
        hbm_in=(0,),
        hbm_out=(0,),
    )
    column = lax.all_to_all(copies, "z", split_axis=0, concat_axis=0, tiled=True)
    column, theirs, pos_theirs = lax.optimization_barrier((column, theirs, pos_theirs))
    column = column.reshape(n, width)
    side = to_sides(column, ny)
    column2 = swapped(column)
    members = ny * nx
    st1, weights, stats = call(
        functools.partial(stat_kernel, scale, rows),
        [((8, count), F32), ((2 * n, count), BF16), ((members, 1, 2 * count), F32)],
        (base, column, column2, queries, pos, theirs, pos_theirs),
        [((2 * n, count), F32), ((2 * n, count), BF16), pltpu.SemaphoreType.DMA],
        4 * flops,
        hbm_out=(1,),
    )
    every = lax.all_to_all(stats, ("yl", *OUTER), split_axis=0, concat_axis=0, tiled=True)
    side2 = swapped(side)
    queries, side, scores = call(
        side_kernel,
        [(queries.shape, BF16), ((n, width), BF16), ((n, count), F32)],
        (queries, side),
        [pltpu.SemaphoreType.DMA((2,))],
        flops,
        vmem=8,
        hbm_in=(0, 1),
    )
    st, m, ch = call(
        functools.partial(mix_kernel, scale, rows),
        [((8, count), F32), ((width, count), F32), ((width, count), BF16)],
        (base, column, column2, weights, side, scores, side2, queries, pos, st1),
        [
            ((n, count), F32),
            ((2 * n, count), BF16),
            ((n, width), BF16),
            ((n, width), BF16),
            ((2 * n, count), BF16),
            pltpu.SemaphoreType.DMA((3,)),
        ],
        10 * flops,
        vmem=24,
        hbm_in=(1, 2, 3),
    )
    out, loss = call(
        functools.partial(scale_kernel, scale),
        [((nx, width // nx, count), BF16), ((1, count), F32)],
        (every, st, m, ch),
    )
    got = lax.all_to_all(out, "x", split_axis=0, concat_axis=0, tiled=True)
    (out,) = call(functools.partial(sum_kernel, 1.0), [((width // nx, count), BF16)], (got,))
    nyh = ny // 2
    piece = width // nx // nyh
    out = out.reshape(nyh, piece, count)
    got = lax.all_to_all(out, "yh", split_axis=0, concat_axis=0, tiled=True)
    (grad,) = call(functools.partial(sum_kernel, scale), [((piece, count), BF16)], (got,))
    return grad.T, loss.reshape(count)


def solution(mesh):
    devices = mesh.devices
    torus = Mesh(devices.reshape(4, 4, 8, 2, 2), ("yh", "x", "z", "yl", "c"))
    in_specs = (P(INNER, None), P((*OUTER, *INNER), None), P(INNER))
    out_specs = (P(INNER, OUTER), P(INNER))
    return jax.shard_map(shards, mesh=torus, in_specs=in_specs, out_specs=out_specs, check_vma=False)
```

```python
import functools
import math

import jax
import jax.numpy as jnp
from jax import lax
from jax.experimental import pallas as pl
from jax.experimental.pallas import tpu as pltpu
from jax.sharding import Mesh
from jax.sharding import PartitionSpec as P


INNER = ("z", "yl", "c")
OUTER = ("yh", "x")
LANE = ("yh", "yl", "c")
F32, BF16 = jnp.float32, jnp.bfloat16
LOG2E = math.log2(math.e)
VMEM = pl.BlockSpec(memory_space=pltpu.VMEM)
SMEM = pl.BlockSpec(memory_space=pltpu.SMEM)
HBM = pl.BlockSpec(memory_space=pltpu.HBM)


def swapped(x):
    return lax.ppermute(x, "c", [(0, 1), (1, 0)])


def to_sides(x, ny):
    perm = []
    for y in range(ny):
        perm.append((2 * y, 2 * ((y - 1) % ny)))
        perm.append((2 * y + 1, 2 * ((y + 1) % ny) + 1))
    return lax.ppermute(x, LANE, perm)


def dot(a, b, dims):
    return lax.dot_general(a, b, (dims, ((), ())), preferred_element_type=F32)


def hits_of(pos_ref, base, count, rows):
    j = lax.broadcasted_iota(jnp.int32, (count, 1), 0)
    return (j // rows) * (4 * rows) + j % rows == pos_ref[...] - base


def statistics(p_refs, bases, q_ref, pos_ref, s_ref, rows):
    q = q_ref[...]
    top = ps = None
    for i, p_ref in enumerate(p_refs):
        n = p_ref.shape[0]
        s = dot(p_ref[...], q, ((1,), (1,)))
        s_ref[i * n : (i + 1) * n, :] = s
        hit = hits_of(pos_ref, bases[i], n, rows)
        t = jnp.max(s, axis=0, keepdims=True)
        u = jnp.sum(jnp.where(hit, s, 0.0), axis=0, keepdims=True)
        top = t if top is None else jnp.maximum(top, t)
        ps = u if ps is None else ps + u
    return top, ps


def products(p_refs, bases, w_ref, pos_ref, rows):
    mix = chosen = 0.0
    for i, p_ref in enumerate(p_refs):
        n = p_ref.shape[0]
        p = p_ref[...]
        hit = hits_of(pos_ref, bases[i], n, rows).astype(F32).astype(BF16)
        mix += dot(p, w_ref[i * n : (i + 1) * n, :], ((0,), (0,)))
        chosen += dot(p, hit, ((0,), (0,)))
    return mix, chosen


def stat_kernel(scale, rows, base_ref, a_ref, b_ref, q_ref, pos_ref, qf_ref, posf_ref, st_ref, w_hbm, out_ref, s_ref, w_ref, sem):
    bases = (base_ref[0], base_ref[1])
    pieces = []
    for qq, pp in ((q_ref, pos_ref), (qf_ref, posf_ref)):
        top, ps = statistics((a_ref, b_ref), bases, qq, pp, s_ref, rows)
        e = jnp.exp2((s_ref[...] - top) * (scale * LOG2E))
        total = jnp.sum(e, axis=0, keepdims=True)
        if not pieces:
            w_ref[...] = e.astype(BF16)
            copy = pltpu.make_async_copy(w_ref, w_hbm, sem)
            copy.start()
            st_ref[0:1, :] = top
        pieces.append(jnp.concatenate([top * scale + jnp.log(total), ps * scale], axis=1))
    own, theirs = pieces
    lower = base_ref[4] == 0
    half = out_ref.shape[0] // 2
    shape = (half, *own.shape)
    out_ref[:half] = jnp.broadcast_to(jnp.where(lower, own, theirs)[None], shape)
    out_ref[half:] = jnp.broadcast_to(jnp.where(lower, theirs, own)[None], shape)
    copy.wait()


def side_kernel(q_hbm, side_hbm, q_ref, side_ref, s_ref, sems):
    pairs = ((q_hbm, q_ref), (side_hbm, side_ref))
    copies = [pltpu.make_async_copy(src, dst, sems.at[i]) for i, (src, dst) in enumerate(pairs)]
    for copy in copies:
        copy.start()
    for copy in copies:
        copy.wait()
    s_ref[...] = dot(side_ref[...], q_ref[...], ((1,), (1,)))


def mix_kernel(scale, rows, base_ref, a_hbm, b_hbm, wo_hbm, side_ref, ss_ref, side2_ref, q_ref, pos_ref, st0_ref, st_ref, m_ref, c_ref, s_ref, w_ref, a_ref, b_ref, wo_ref, sems):
    pairs = ((a_hbm, a_ref), (b_hbm, b_ref), (wo_hbm, wo_ref))
    copies = [pltpu.make_async_copy(src, dst, sems.at[i]) for i, (src, dst) in enumerate(pairs)]
    for copy in copies:
        copy.start()
    n = side2_ref.shape[0]
    k = scale * LOG2E
    s_ref[...] = dot(side2_ref[...], q_ref[...], ((1,), (1,)))
    top0 = st0_ref[0:1, :]
    top = jnp.maximum(jnp.max(s_ref[...], axis=0, keepdims=True), jnp.max(ss_ref[...], axis=0, keepdims=True))
    top = jnp.maximum(top, top0)
    st_ref[0:1, :] = top
    w_ref[:n, :] = jnp.exp2((s_ref[...] - top) * k).astype(BF16)
    w_ref[n:, :] = jnp.exp2((ss_ref[...] - top) * k).astype(BF16)
    mix, chosen = products((side2_ref, side_ref), (base_ref[3], base_ref[2]), w_ref, pos_ref, rows)
    m_ref[...] = mix
    for copy in copies:
        copy.wait()
    mix, more = products((a_ref, b_ref), (base_ref[0], base_ref[1]), wo_ref, pos_ref, rows)
    m_ref[...] += mix * jnp.exp2((top0 - top) * k)
    c_ref[...] = (chosen + more).astype(BF16)


def scale_kernel(scale, every_ref, st_ref, m_ref, c_ref, out_ref, loss_ref):
    count = m_ref.shape[1]
    lse = every_ref[:, 0, :count]
    most = jnp.max(lse, axis=0, keepdims=True)
    whole = most + jnp.log(jnp.sum(jnp.exp(lse - most), axis=0, keepdims=True))
    ps = jnp.sum(every_ref[:, 0, count:], axis=0, keepdims=True)
    g = jnp.exp(st_ref[0:1, :] * scale - whole)
    out = (m_ref[...] * g - c_ref[...].astype(F32)).astype(BF16)
    nx, width, _ = out_ref.shape
    piece = width // 4
    for i in range(nx):
        for j in range(4):
            at = (j * nx + i) * piece
            out_ref[i, j * piece : (j + 1) * piece, :] = out[at : at + piece]
    loss_ref[...] = whole - ps


def copy_kernel(x_hbm, out_hbm, x_ref, sems):
    n = out_hbm.shape[0]
    first = pltpu.make_async_copy(x_hbm, x_ref, sems.at[n])
    first.start()
    first.wait()
    copies = [pltpu.make_async_copy(x_ref, out_hbm.at[i], sems.at[i]) for i in range(n)]
    for copy in copies:
        copy.start()
    for copy in copies:
        copy.wait()


def middle_kernel(base_ref, got_ref, *refs):
    outs, sum_ref = refs[:-1], refs[-1]
    total = got_ref[0].astype(F32)
    for i in range(1, got_ref.shape[0]):
        total += got_ref[i].astype(F32)
    sum_ref[...] = total
    n, piece = len(outs), outs[0].shape[0]
    for k in range(n):
        at = pl.multiple_of(((base_ref[5] + k) & (n - 1)) * piece, 8)
        outs[k][...] = sum_ref[pl.ds(at, piece), :].astype(BF16)


def final_kernel(scale, *refs):
    total = refs[0][...].astype(F32)
    for ref in refs[1:-1]:
        total += ref[...].astype(F32)
    refs[-1][...] = (scale * total).astype(BF16)


def call(body, out, operands, scratch=(), flops=0, vmem=12, hbm_in=(), hbm_out=()):
    def spec(i, o):
        if i in hbm_in:
            return HBM
        return SMEM if o.dtype == jnp.int32 and o.ndim == 1 else VMEM

    kernel = pl.pallas_call(
        body,
        in_specs=[spec(i, o) for i, o in enumerate(operands)],
        out_specs=[HBM if i in hbm_out else VMEM for i in range(len(out))],
        out_shape=[pltpu.HBM(s, d) if i in hbm_out else jax.ShapeDtypeStruct(s, d) for i, (s, d) in enumerate(out)],
        scratch_shapes=[s if not isinstance(s, tuple) else pltpu.VMEM(*s) for s in scratch],
        cost_estimate=pl.CostEstimate(flops=flops, bytes_accessed=4 << 20, transcendentals=0),
        compiler_params=pltpu.CompilerParams(vmem_limit_bytes=vmem << 20),
    )
    operands = [pltpu.with_memory_space_constraint(o, pltpu.HBM) if i in hbm_in else o for i, o in enumerate(operands)]
    return kernel(*operands)


def shards(queries, passages, positive):
    count, width = queries.shape
    rows = passages.shape[0]
    scale = 3.0 / math.sqrt(width)
    nz, nx = lax.axis_size("z"), lax.axis_size("x")
    ny = lax.axis_size("yh") * 2
    x, c = lax.axis_index("x"), lax.axis_index("c")
    y = lax.axis_index("yh") * 2 + lax.axis_index("yl")
    n = nz * rows
    flops = 2 * n * width * count

    def base_of(yy, cc):
        yy = (yy + ny) & (ny - 1)
        return ((((yy >> 1) * nx + x) * nz * 2 + (yy & 1)) * 2 + cc) * rows

    base = jnp.stack(
        [base_of(y, c), base_of(y, 1 - c), base_of(y + 1 - 2 * c, c), base_of(y - 1 + 2 * c, 1 - c), y & 1, y >> 1]
    )
    pos = positive.reshape(1, count)

    theirs = to_sides(queries, ny)
    pos_theirs = to_sides(pos, ny)
    (copies,) = call(
        copy_kernel,
        [((nz, rows, width), BF16)],
        (passages,),
        [((rows, width), BF16), pltpu.SemaphoreType.DMA((nz + 1,))],
        hbm_in=(0,),
        hbm_out=(0,),
    )
    column = lax.all_to_all(copies, "z", split_axis=0, concat_axis=0, tiled=True)
    column, theirs, pos_theirs = lax.optimization_barrier((column, theirs, pos_theirs))
    column = column.reshape(n, width)
    side = to_sides(column, ny)
    column2 = swapped(column)
    members = ny * nx
    st1, weights, stats = call(
        functools.partial(stat_kernel, scale, rows),
        [((8, count), F32), ((2 * n, count), BF16), ((members, 1, 2 * count), F32)],
        (base, column, column2, queries, pos, theirs, pos_theirs),
        [((2 * n, count), F32), ((2 * n, count), BF16), pltpu.SemaphoreType.DMA],
        4 * flops,
        hbm_out=(1,),
    )
    every = lax.all_to_all(stats, ("yl", *OUTER), split_axis=0, concat_axis=0, tiled=True)
    side2 = swapped(side)
    queries, side, scores = call(
        side_kernel,
        [(queries.shape, BF16), ((n, width), BF16), ((n, count), F32)],
        (queries, side),
        [pltpu.SemaphoreType.DMA((2,))],
        flops,
        vmem=8,
        hbm_in=(0, 1),
    )
    st, m, ch = call(
        functools.partial(mix_kernel, scale, rows),
        [((8, count), F32), ((width, count), F32), ((width, count), BF16)],
        (base, column, column2, weights, side, scores, side2, queries, pos, st1),
        [
            ((n, count), F32),
            ((2 * n, count), BF16),
            ((n, width), BF16),
            ((n, width), BF16),
            ((2 * n, count), BF16),
            pltpu.SemaphoreType.DMA((3,)),
        ],
        10 * flops,
        vmem=24,
        hbm_in=(1, 2, 3),
    )
    out, loss = call(
        functools.partial(scale_kernel, scale),
        [((nx, width // nx, count), BF16), ((1, count), F32)],
        (every, st, m, ch),
    )
    got = lax.all_to_all(out, "x", split_axis=0, concat_axis=0, tiled=True)
    nyh = ny // 2
    piece = width // nx // nyh
    pieces = call(middle_kernel, [((piece, count), BF16)] * nyh, (base, got), [((width // nx, count), F32)])
    got = [pieces[0]]
    for k in range(1, nyh):
        got.append(lax.ppermute(pieces[k], "yh", [(i, (i + k) % nyh) for i in range(nyh)]))
    (grad,) = call(functools.partial(final_kernel, scale), [((piece, count), BF16)], got)
    return grad.T, loss.reshape(count)


def solution(mesh):
    devices = mesh.devices
    torus = Mesh(devices.reshape(4, 4, 8, 2, 2), ("yh", "x", "z", "yl", "c"))
    in_specs = (P(INNER, None), P((*OUTER, *INNER), None), P(INNER))
    out_specs = (P(INNER, OUTER), P(INNER))
    return jax.shard_map(shards, mesh=torus, in_specs=in_specs, out_specs=out_specs, check_vma=False)
```

```python
import functools
import math

import jax
import jax.numpy as jnp
from jax import lax
from jax.experimental import pallas as pl
from jax.experimental.pallas import tpu as pltpu
from jax.sharding import Mesh
from jax.sharding import PartitionSpec as P


INNER = ("z", "yl", "c")
OUTER = ("yh", "x")
LANE = ("yh", "yl", "c")
F32, BF16 = jnp.float32, jnp.bfloat16
LOG2E = math.log2(math.e)
VMEM = pl.BlockSpec(memory_space=pltpu.VMEM)
SMEM = pl.BlockSpec(memory_space=pltpu.SMEM)
HBM = pl.BlockSpec(memory_space=pltpu.HBM)


def swapped(x):
    return lax.ppermute(x, "c", [(0, 1), (1, 0)])


def to_sides(x, ny):
    perm = []
    for y in range(ny):
        perm.append((2 * y, 2 * ((y + 1) % ny)))
        perm.append((2 * y + 1, 2 * ((y - 1) % ny) + 1))
    return lax.ppermute(x, LANE, perm)


def dot(a, b, dims):
    return lax.dot_general(a, b, (dims, ((), ())), preferred_element_type=F32)


def hits_of(pos_ref, base, count, rows):
    j = lax.broadcasted_iota(jnp.int32, (count, 1), 0)
    return (j // rows) * (4 * rows) + j % rows == pos_ref[...] - base


def statistics(p_refs, bases, q_ref, pos_ref, s_ref, rows):
    q = q_ref[...]
    top = ps = None
    for i, p_ref in enumerate(p_refs):
        n = p_ref.shape[0]
        s = dot(p_ref[...], q, ((1,), (1,)))
        s_ref[i * n : (i + 1) * n, :] = s
        hit = hits_of(pos_ref, bases[i], n, rows)
        t = jnp.max(s, axis=0, keepdims=True)
        u = jnp.sum(jnp.where(hit, s, 0.0), axis=0, keepdims=True)
        top = t if top is None else jnp.maximum(top, t)
        ps = u if ps is None else ps + u
    return top, ps


def products(p_refs, bases, w_ref, pos_ref, rows):
    mix = chosen = 0.0
    for i, p_ref in enumerate(p_refs):
        n = p_ref.shape[0]
        p = p_ref[...]
        hit = hits_of(pos_ref, bases[i], n, rows).astype(F32).astype(BF16)
        mix += dot(p, w_ref[i * n : (i + 1) * n, :], ((0,), (0,)))
        chosen += dot(p, hit, ((0,), (0,)))
    return mix, chosen


def stat_kernel(scale, rows, base_ref, a_ref, b_ref, q_ref, pos_ref, qf_ref, posf_ref, st_ref, w_hbm, out_ref, s_ref, w_ref, sem):
    bases = (base_ref[0], base_ref[1])
    pieces = []
    for qq, pp in ((q_ref, pos_ref), (qf_ref, posf_ref)):
        top, ps = statistics((a_ref, b_ref), bases, qq, pp, s_ref, rows)
        e = jnp.exp2((s_ref[...] - top) * (scale * LOG2E))
        total = jnp.sum(e, axis=0, keepdims=True)
        if not pieces:
            w_ref[...] = e.astype(BF16)
            copy = pltpu.make_async_copy(w_ref, w_hbm, sem)
            copy.start()
            st_ref[0:1, :] = top
        pieces.append(jnp.concatenate([top * scale + jnp.log(total), ps * scale], axis=1))
    own, theirs = pieces
    lower = base_ref[4] == 0
    half = out_ref.shape[0] // 2
    shape = (half, *own.shape)
    out_ref[:half] = jnp.broadcast_to(jnp.where(lower, own, theirs)[None], shape)
    out_ref[half:] = jnp.broadcast_to(jnp.where(lower, theirs, own)[None], shape)
    copy.wait()


def side_kernel(q_hbm, side_hbm, q_ref, side_ref, s_ref, sems):
    pairs = ((q_hbm, q_ref), (side_hbm, side_ref))
    copies = [pltpu.make_async_copy(src, dst, sems.at[i]) for i, (src, dst) in enumerate(pairs)]
    for copy in copies:
        copy.start()
    for copy in copies:
        copy.wait()
    s_ref[...] = dot(side_ref[...], q_ref[...], ((1,), (1,)))


def mix_kernel(scale, rows, base_ref, a_hbm, b_hbm, wo_hbm, side_ref, ss_ref, side2_ref, q_ref, pos_ref, st0_ref, st_ref, m_ref, c_ref, s_ref, w_ref, a_ref, b_ref, wo_ref, sems):
    pairs = ((a_hbm, a_ref), (b_hbm, b_ref), (wo_hbm, wo_ref))
    copies = [pltpu.make_async_copy(src, dst, sems.at[i]) for i, (src, dst) in enumerate(pairs)]
    for copy in copies:
        copy.start()
    n = side2_ref.shape[0]
    k = scale * LOG2E
    s_ref[...] = dot(side2_ref[...], q_ref[...], ((1,), (1,)))
    top0 = st0_ref[0:1, :]
    top = jnp.maximum(jnp.max(s_ref[...], axis=0, keepdims=True), jnp.max(ss_ref[...], axis=0, keepdims=True))
    top = jnp.maximum(top, top0)
    st_ref[0:1, :] = top
    w_ref[:n, :] = jnp.exp2((s_ref[...] - top) * k).astype(BF16)
    w_ref[n:, :] = jnp.exp2((ss_ref[...] - top) * k).astype(BF16)
    mix, chosen = products((side2_ref, side_ref), (base_ref[3], base_ref[2]), w_ref, pos_ref, rows)
    m_ref[...] = mix
    for copy in copies:
        copy.wait()
    mix, more = products((a_ref, b_ref), (base_ref[0], base_ref[1]), wo_ref, pos_ref, rows)
    m_ref[...] += mix * jnp.exp2((top0 - top) * k)
    c_ref[...] = (chosen + more).astype(BF16)


def scale_kernel(scale, every_ref, st_ref, m_ref, c_ref, out_ref, loss_ref):
    count = m_ref.shape[1]
    lse = every_ref[:, 0, :count]
    most = jnp.max(lse, axis=0, keepdims=True)
    whole = most + jnp.log(jnp.sum(jnp.exp(lse - most), axis=0, keepdims=True))
    ps = jnp.sum(every_ref[:, 0, count:], axis=0, keepdims=True)
    g = jnp.exp(st_ref[0:1, :] * scale - whole)
    out = (m_ref[...] * g - c_ref[...].astype(F32)).astype(BF16)
    nx, width, _ = out_ref.shape
    piece = width // 4
    for i in range(nx):
        for j in range(4):
            at = (j * nx + i) * piece
            out_ref[i, j * piece : (j + 1) * piece, :] = out[at : at + piece]
    loss_ref[...] = whole - ps


def copy_kernel(x_hbm, out_hbm, x_ref, sems):
    n = out_hbm.shape[0]
    first = pltpu.make_async_copy(x_hbm, x_ref, sems.at[n])
    first.start()
    first.wait()
    copies = [pltpu.make_async_copy(x_ref, out_hbm.at[i], sems.at[i]) for i in range(n)]
    for copy in copies:
        copy.start()
    for copy in copies:
        copy.wait()


def sum_kernel(scale, got_ref, out_ref):
    total = got_ref[0].astype(F32)
    for i in range(1, got_ref.shape[0]):
        total += got_ref[i].astype(F32)
    out_ref[...] = (scale * total).astype(BF16)


def call(body, out, operands, scratch=(), flops=0, vmem=12, hbm_in=(), hbm_out=()):
    def spec(i, o):
        if i in hbm_in:
            return HBM
        return SMEM if o.dtype == jnp.int32 and o.ndim == 1 else VMEM

    kernel = pl.pallas_call(
        body,
        in_specs=[spec(i, o) for i, o in enumerate(operands)],
        out_specs=[HBM if i in hbm_out else VMEM for i in range(len(out))],
        out_shape=[pltpu.HBM(s, d) if i in hbm_out else jax.ShapeDtypeStruct(s, d) for i, (s, d) in enumerate(out)],
        scratch_shapes=[s if not isinstance(s, tuple) else pltpu.VMEM(*s) for s in scratch],
        cost_estimate=pl.CostEstimate(flops=flops, bytes_accessed=4 << 20, transcendentals=0),
        compiler_params=pltpu.CompilerParams(vmem_limit_bytes=vmem << 20),
    )
    operands = [pltpu.with_memory_space_constraint(o, pltpu.HBM) if i in hbm_in else o for i, o in enumerate(operands)]
    return kernel(*operands)


def shards(queries, passages, positive):
    count, width = queries.shape
    rows = passages.shape[0]
    scale = 3.0 / math.sqrt(width)
    nz, nx = lax.axis_size("z"), lax.axis_size("x")
    ny = lax.axis_size("yh") * 2
    x, c = lax.axis_index("x"), lax.axis_index("c")
    y = lax.axis_index("yh") * 2 + lax.axis_index("yl")
    n = nz * rows
    flops = 2 * n * width * count

    def base_of(yy, cc):
        yy = (yy + ny) & (ny - 1)
        return ((((yy >> 1) * nx + x) * nz * 2 + (yy & 1)) * 2 + cc) * rows

    base = jnp.stack(
        [base_of(y, c), base_of(y, 1 - c), base_of(y - 1 + 2 * c, c), base_of(y + 1 - 2 * c, 1 - c), y & 1]
    )
    pos = positive.reshape(1, count)

    theirs = to_sides(queries, ny)
    pos_theirs = to_sides(pos, ny)
    (copies,) = call(
        copy_kernel,
        [((nz, rows, width), BF16)],
        (passages,),
        [((rows, width), BF16), pltpu.SemaphoreType.DMA((nz + 1,))],
        hbm_in=(0,),
        hbm_out=(0,),
    )
    column = lax.all_to_all(copies, "z", split_axis=0, concat_axis=0, tiled=True)
    column, theirs, pos_theirs = lax.optimization_barrier((column, theirs, pos_theirs))
    column = column.reshape(n, width)
    side = to_sides(column, ny)
    column2 = swapped(column)
    members = ny * nx
    st1, weights, stats = call(
        functools.partial(stat_kernel, scale, rows),
        [((8, count), F32), ((2 * n, count), BF16), ((members, 1, 2 * count), F32)],
        (base, column, column2, queries, pos, theirs, pos_theirs),
        [((2 * n, count), F32), ((2 * n, count), BF16), pltpu.SemaphoreType.DMA],
        4 * flops,
        hbm_out=(1,),
    )
    every = lax.all_to_all(stats, ("yl", *OUTER), split_axis=0, concat_axis=0, tiled=True)
    side2 = swapped(side)
    queries, side, scores = call(
        side_kernel,
        [(queries.shape, BF16), ((n, width), BF16), ((n, count), F32)],
        (queries, side),
        [pltpu.SemaphoreType.DMA((2,))],
        flops,
        vmem=8,
        hbm_in=(0, 1),
    )
    st, m, ch = call(
        functools.partial(mix_kernel, scale, rows),
        [((8, count), F32), ((width, count), F32), ((width, count), BF16)],
        (base, column, column2, weights, side, scores, side2, queries, pos, st1),
        [
            ((n, count), F32),
            ((2 * n, count), BF16),
            ((n, width), BF16),
            ((n, width), BF16),
            ((2 * n, count), BF16),
            pltpu.SemaphoreType.DMA((3,)),
        ],
        10 * flops,
        vmem=24,
        hbm_in=(1, 2, 3),
    )
    out, loss = call(
        functools.partial(scale_kernel, scale),
        [((nx, width // nx, count), BF16), ((1, count), F32)],
        (every, st, m, ch),
    )
    got = lax.all_to_all(out, "x", split_axis=0, concat_axis=0, tiled=True)
    (out,) = call(functools.partial(sum_kernel, 1.0), [((width // nx, count), BF16)], (got,))
    nyh = ny // 2
    piece = width // nx // nyh
    out = out.reshape(nyh, piece, count)
    got = lax.all_to_all(out, "yh", split_axis=0, concat_axis=0, tiled=True)
    (grad,) = call(functools.partial(sum_kernel, scale), [((piece, count), BF16)], (got,))
    return grad.T, loss.reshape(count)


def solution(mesh):
    devices = mesh.devices
    torus = Mesh(devices.reshape(4, 4, 8, 2, 2), ("yh", "x", "z", "yl", "c"))
    in_specs = (P(INNER, None), P((*OUTER, *INNER), None), P(INNER))
    out_specs = (P(INNER, OUTER), P(INNER))
    return jax.shard_map(shards, mesh=torus, in_specs=in_specs, out_specs=out_specs, check_vma=False)
```

```python
import functools
import math

import jax
import jax.numpy as jnp
from jax import lax
from jax.experimental import pallas as pl
from jax.experimental.pallas import tpu as pltpu
from jax.sharding import Mesh
from jax.sharding import PartitionSpec as P


INNER = ("z", "yl", "c")
OUTER = ("yh", "x")
LANE = ("yh", "yl", "c")
F32, BF16 = jnp.float32, jnp.bfloat16
LOG2E = math.log2(math.e)
VMEM = pl.BlockSpec(memory_space=pltpu.VMEM)
SMEM = pl.BlockSpec(memory_space=pltpu.SMEM)
HBM = pl.BlockSpec(memory_space=pltpu.HBM)


def swapped(x):
    return lax.ppermute(x, "c", [(0, 1), (1, 0)])


def to_sides(x, ny):
    perm = []
    for y in range(ny):
        perm.append((2 * y, 2 * ((y + 1) % ny)))
        perm.append((2 * y + 1, 2 * ((y - 1) % ny) + 1))
    return lax.ppermute(x, LANE, perm)


def dot(a, b, dims):
    return lax.dot_general(a, b, (dims, ((), ())), preferred_element_type=F32)


def hits_of(pos_ref, base, count, rows):
    j = lax.broadcasted_iota(jnp.int32, (count, 1), 0)
    return (j // rows) * (4 * rows) + j % rows == pos_ref[...] - base


def statistics(p_refs, bases, q_ref, pos_ref, s_ref, rows):
    q = q_ref[...]
    top = ps = None
    for i, p_ref in enumerate(p_refs):
        n = p_ref.shape[0]
        s = dot(p_ref[...], q, ((1,), (1,)))
        s_ref[i * n : (i + 1) * n, :] = s
        hit = hits_of(pos_ref, bases[i], n, rows)
        t = jnp.max(s, axis=0, keepdims=True)
        u = jnp.sum(jnp.where(hit, s, 0.0), axis=0, keepdims=True)
        top = t if top is None else jnp.maximum(top, t)
        ps = u if ps is None else ps + u
    return top, ps


def products(p_refs, bases, w_ref, pos_ref, rows):
    mix = chosen = 0.0
    for i, p_ref in enumerate(p_refs):
        n = p_ref.shape[0]
        p = p_ref[...]
        hit = hits_of(pos_ref, bases[i], n, rows).astype(F32).astype(BF16)
        mix += dot(p, w_ref[i * n : (i + 1) * n, :], ((0,), (0,)))
        chosen += dot(p, hit, ((0,), (0,)))
    return mix, chosen


def stat_kernel(scale, rows, base_ref, a_ref, b_ref, q_ref, pos_ref, qf_ref, posf_ref, st_ref, w_hbm, out_ref, s_ref, w_ref, sem):
    bases = (base_ref[0], base_ref[1])
    pieces = []
    for qq, pp in ((q_ref, pos_ref), (qf_ref, posf_ref)):
        top, ps = statistics((a_ref, b_ref), bases, qq, pp, s_ref, rows)
        e = jnp.exp2((s_ref[...] - top) * (scale * LOG2E))
        total = jnp.sum(e, axis=0, keepdims=True)
        if not pieces:
            w_ref[...] = e.astype(BF16)
            copy = pltpu.make_async_copy(w_ref, w_hbm, sem)
            copy.start()
            st_ref[0:1, :] = top
        pieces.append(jnp.concatenate([top * scale + jnp.log(total), ps * scale], axis=1))
    own, theirs = pieces
    lower = base_ref[4] == 0
    half = out_ref.shape[0] // 2
    shape = (half, *own.shape)
    out_ref[:half] = jnp.broadcast_to(jnp.where(lower, own, theirs)[None], shape)
    out_ref[half:] = jnp.broadcast_to(jnp.where(lower, theirs, own)[None], shape)
    copy.wait()


def side_kernel(q_hbm, side_hbm, q_ref, side_ref, s_ref, sems):
    pairs = ((q_hbm, q_ref), (side_hbm, side_ref))
    copies = [pltpu.make_async_copy(src, dst, sems.at[i]) for i, (src, dst) in enumerate(pairs)]
    for copy in copies:
        copy.start()
    for copy in copies:
        copy.wait()
    s_ref[...] = dot(side_ref[...], q_ref[...], ((1,), (1,)))


def mix_kernel(scale, rows, base_ref, a_hbm, b_hbm, wo_hbm, side_ref, ss_ref, side2_ref, q_ref, pos_ref, st0_ref, st_ref, m_ref, c_ref, s_ref, w_ref, a_ref, b_ref, wo_ref, sems):
    pairs = ((a_hbm, a_ref), (b_hbm, b_ref), (wo_hbm, wo_ref))
    copies = [pltpu.make_async_copy(src, dst, sems.at[i]) for i, (src, dst) in enumerate(pairs)]
    for copy in copies:
        copy.start()
    n = side2_ref.shape[0]
    k = scale * LOG2E
    s_ref[...] = dot(side2_ref[...], q_ref[...], ((1,), (1,)))
    top0 = st0_ref[0:1, :]
    top = jnp.maximum(jnp.max(s_ref[...], axis=0, keepdims=True), jnp.max(ss_ref[...], axis=0, keepdims=True))
    top = jnp.maximum(top, top0)
    st_ref[0:1, :] = top
    w_ref[:n, :] = jnp.exp2((s_ref[...] - top) * k).astype(BF16)
    w_ref[n:, :] = jnp.exp2((ss_ref[...] - top) * k).astype(BF16)
    mix, chosen = products((side2_ref, side_ref), (base_ref[3], base_ref[2]), w_ref, pos_ref, rows)
    m_ref[...] = mix
    for copy in copies:
        copy.wait()
    mix, more = products((a_ref, b_ref), (base_ref[0], base_ref[1]), wo_ref, pos_ref, rows)
    m_ref[...] += mix * jnp.exp2((top0 - top) * k)
    c_ref[...] = (chosen + more).astype(BF16)


def scale_kernel(scale, every_ref, st_ref, m_ref, c_ref, out_ref, loss_ref):
    count = m_ref.shape[1]
    lse = every_ref[:, 0, :count]
    most = jnp.max(lse, axis=0, keepdims=True)
    whole = most + jnp.log(jnp.sum(jnp.exp(lse - most), axis=0, keepdims=True))
    ps = jnp.sum(every_ref[:, 0, count:], axis=0, keepdims=True)
    g = jnp.exp(st_ref[0:1, :] * scale - whole)
    out = (m_ref[...] * g - c_ref[...].astype(F32)).astype(BF16)
    nx, width, _ = out_ref.shape
    piece = width // 4
    for i in range(nx):
        for j in range(4):
            at = (j * nx + i) * piece
            out_ref[i, j * piece : (j + 1) * piece, :] = out[at : at + piece]
    loss_ref[...] = whole - ps


def copy_kernel(x_hbm, out_hbm, sems):
    n = out_hbm.shape[0]
    copies = [pltpu.make_async_copy(x_hbm, out_hbm.at[i], sems.at[i]) for i in range(n)]
    for copy in copies:
        copy.start()
    for copy in copies:
        copy.wait()


def sum_kernel(scale, got_ref, out_ref):
    total = got_ref[0].astype(F32)
    for i in range(1, got_ref.shape[0]):
        total += got_ref[i].astype(F32)
    out_ref[...] = (scale * total).astype(BF16)


def call(body, out, operands, scratch=(), flops=0, vmem=12, hbm_in=(), hbm_out=()):
    def spec(i, o):
        if i in hbm_in:
            return HBM
        return SMEM if o.dtype == jnp.int32 and o.ndim == 1 else VMEM

    kernel = pl.pallas_call(
        body,
        in_specs=[spec(i, o) for i, o in enumerate(operands)],
        out_specs=[HBM if i in hbm_out else VMEM for i in range(len(out))],
        out_shape=[pltpu.HBM(s, d) if i in hbm_out else jax.ShapeDtypeStruct(s, d) for i, (s, d) in enumerate(out)],
        scratch_shapes=[s if not isinstance(s, tuple) else pltpu.VMEM(*s) for s in scratch],
        cost_estimate=pl.CostEstimate(flops=flops, bytes_accessed=4 << 20, transcendentals=0),
        compiler_params=pltpu.CompilerParams(vmem_limit_bytes=vmem << 20),
    )
    operands = [pltpu.with_memory_space_constraint(o, pltpu.HBM) if i in hbm_in else o for i, o in enumerate(operands)]
    return kernel(*operands)


def shards(queries, passages, positive):
    count, width = queries.shape
    rows = passages.shape[0]
    scale = 3.0 / math.sqrt(width)
    nz, nx = lax.axis_size("z"), lax.axis_size("x")
    ny = lax.axis_size("yh") * 2
    x, c = lax.axis_index("x"), lax.axis_index("c")
    y = lax.axis_index("yh") * 2 + lax.axis_index("yl")
    n = nz * rows
    flops = 2 * n * width * count

    def base_of(yy, cc):
        yy = (yy + ny) & (ny - 1)
        return ((((yy >> 1) * nx + x) * nz * 2 + (yy & 1)) * 2 + cc) * rows

    base = jnp.stack(
        [base_of(y, c), base_of(y, 1 - c), base_of(y - 1 + 2 * c, c), base_of(y + 1 - 2 * c, 1 - c), y & 1]
    )
    pos = positive.reshape(1, count)

    theirs = to_sides(queries, ny)
    pos_theirs = to_sides(pos, ny)
    (copies,) = call(
        copy_kernel,
        [((nz, rows, width), BF16)],
        (passages,),
        [pltpu.SemaphoreType.DMA((nz,))],
        hbm_in=(0,),
        hbm_out=(0,),
    )
    column = lax.all_to_all(copies, "z", split_axis=0, concat_axis=0, tiled=True)
    column, theirs, pos_theirs = lax.optimization_barrier((column, theirs, pos_theirs))
    column = column.reshape(n, width)
    side = to_sides(column, ny)
    column2 = swapped(column)
    members = ny * nx
    st1, weights, stats = call(
        functools.partial(stat_kernel, scale, rows),
        [((8, count), F32), ((2 * n, count), BF16), ((members, 1, 2 * count), F32)],
        (base, column, column2, queries, pos, theirs, pos_theirs),
        [((2 * n, count), F32), ((2 * n, count), BF16), pltpu.SemaphoreType.DMA],
        4 * flops,
        hbm_out=(1,),
    )
    every = lax.all_to_all(stats, ("yl", *OUTER), split_axis=0, concat_axis=0, tiled=True)
    side2 = swapped(side)
    queries, side, scores = call(
        side_kernel,
        [(queries.shape, BF16), ((n, width), BF16), ((n, count), F32)],
        (queries, side),
        [pltpu.SemaphoreType.DMA((2,))],
        flops,
        vmem=8,
        hbm_in=(0, 1),
    )
    st, m, ch = call(
        functools.partial(mix_kernel, scale, rows),
        [((8, count), F32), ((width, count), F32), ((width, count), BF16)],
        (base, column, column2, weights, side, scores, side2, queries, pos, st1),
        [
            ((n, count), F32),
            ((2 * n, count), BF16),
            ((n, width), BF16),
            ((n, width), BF16),
            ((2 * n, count), BF16),
            pltpu.SemaphoreType.DMA((3,)),
        ],
        10 * flops,
        vmem=24,
        hbm_in=(1, 2, 3),
    )
    out, loss = call(
        functools.partial(scale_kernel, scale),
        [((nx, width // nx, count), BF16), ((1, count), F32)],
        (every, st, m, ch),
    )
    got = lax.all_to_all(out, "x", split_axis=0, concat_axis=0, tiled=True)
    (out,) = call(functools.partial(sum_kernel, 1.0), [((width // nx, count), BF16)], (got,))
    nyh = ny // 2
    piece = width // nx // nyh
    out = out.reshape(nyh, piece, count)
    got = lax.all_to_all(out, "yh", split_axis=0, concat_axis=0, tiled=True)
    (grad,) = call(functools.partial(sum_kernel, scale), [((piece, count), BF16)], (got,))
    return grad.T, loss.reshape(count)


def solution(mesh):
    devices = mesh.devices
    torus = Mesh(devices.reshape(4, 4, 8, 2, 2), ("yh", "x", "z", "yl", "c"))
    in_specs = (P(INNER, None), P((*OUTER, *INNER), None), P(INNER))
    out_specs = (P(INNER, OUTER), P(INNER))
    return jax.shard_map(shards, mesh=torus, in_specs=in_specs, out_specs=out_specs, check_vma=False)
```

```python
import functools
import math

import jax
import jax.numpy as jnp
from jax import lax
from jax.experimental import pallas as pl
from jax.experimental.pallas import tpu as pltpu
from jax.sharding import Mesh
from jax.sharding import PartitionSpec as P


INNER = ("z", "yl", "c")
OUTER = ("yh", "x")
LANE = ("yh", "yl", "c")
F32, BF16 = jnp.float32, jnp.bfloat16
LOG2E = math.log2(math.e)
VMEM = pl.BlockSpec(memory_space=pltpu.VMEM)
SMEM = pl.BlockSpec(memory_space=pltpu.SMEM)
HBM = pl.BlockSpec(memory_space=pltpu.HBM)


def swapped(x):
    return lax.ppermute(x, "c", [(0, 1), (1, 0)])


def to_sides(x, ny):
    perm = []
    for y in range(ny):
        perm.append((2 * y, 2 * ((y + 1) % ny)))
        perm.append((2 * y + 1, 2 * ((y - 1) % ny) + 1))
    return lax.ppermute(x, LANE, perm)


def dot(a, b, dims):
    return lax.dot_general(a, b, (dims, ((), ())), preferred_element_type=F32)


def hits_of(pos_ref, base, count, rows):
    j = lax.broadcasted_iota(jnp.int32, (count, 1), 0)
    return (j // rows) * (4 * rows) + j % rows == pos_ref[...] - base


def statistics(p_refs, bases, q_ref, pos_ref, s_ref, rows):
    q = q_ref[...]
    top = ps = None
    for i, p_ref in enumerate(p_refs):
        n = p_ref.shape[0]
        s = dot(p_ref[...], q, ((1,), (1,)))
        s_ref[i * n : (i + 1) * n, :] = s
        hit = hits_of(pos_ref, bases[i], n, rows)
        t = jnp.max(s, axis=0, keepdims=True)
        u = jnp.sum(jnp.where(hit, s, 0.0), axis=0, keepdims=True)
        top = t if top is None else jnp.maximum(top, t)
        ps = u if ps is None else ps + u
    return top, ps


def products(p_refs, bases, w_ref, pos_ref, rows):
    mix = chosen = 0.0
    for i, p_ref in enumerate(p_refs):
        n = p_ref.shape[0]
        p = p_ref[...]
        hit = hits_of(pos_ref, bases[i], n, rows).astype(F32).astype(BF16)
        mix += dot(p, w_ref[i * n : (i + 1) * n, :], ((0,), (0,)))
        chosen += dot(p, hit, ((0,), (0,)))
    return mix, chosen


def stat_kernel(scale, rows, base_ref, a_ref, b_ref, q_ref, pos_ref, qf_ref, posf_ref, st_ref, w_hbm, out_hbm, s_ref, w_ref, row_ref, sems):
    bases = (base_ref[0], base_ref[1])
    half = out_hbm.shape[0] // 2
    lower = jnp.where(base_ref[4] == 0, 0, half)
    copies = []
    for i, (qq, pp) in enumerate(((q_ref, pos_ref), (qf_ref, posf_ref))):
        top, ps = statistics((a_ref, b_ref), bases, qq, pp, s_ref, rows)
        e = jnp.exp2((s_ref[...] - top) * (scale * LOG2E))
        total = jnp.sum(e, axis=0, keepdims=True)
        row_ref[i, :, :] = jnp.concatenate([top * scale + jnp.log(total), ps * scale], axis=1)
        first = lower if i == 0 else half - lower
        for k in range(half):
            copies.append(pltpu.make_async_copy(row_ref.at[i], out_hbm.at[first + k], sems.at[i * half + k]))
            copies[-1].start()
        if i == 0:
            w_ref[...] = e.astype(BF16)
            copies.append(pltpu.make_async_copy(w_ref, w_hbm, sems.at[2 * half]))
            copies[-1].start()
            st_ref[0:1, :] = top
    for copy in copies:
        copy.wait()


def side_kernel(q_hbm, side_hbm, q_ref, side_ref, s_ref, sems):
    pairs = ((q_hbm, q_ref), (side_hbm, side_ref))
    copies = [pltpu.make_async_copy(src, dst, sems.at[i]) for i, (src, dst) in enumerate(pairs)]
    for copy in copies:
        copy.start()
    for copy in copies:
        copy.wait()
    s_ref[...] = dot(side_ref[...], q_ref[...], ((1,), (1,)))


def mix_kernel(scale, rows, base_ref, a_hbm, b_hbm, wo_hbm, side_ref, ss_ref, side2_ref, q_ref, pos_ref, st0_ref, st_ref, m_ref, c_ref, s_ref, w_ref, a_ref, b_ref, wo_ref, sems):
    pairs = ((a_hbm, a_ref), (b_hbm, b_ref), (wo_hbm, wo_ref))
    copies = [pltpu.make_async_copy(src, dst, sems.at[i]) for i, (src, dst) in enumerate(pairs)]
    for copy in copies:
        copy.start()
    n = side2_ref.shape[0]
    k = scale * LOG2E
    s_ref[...] = dot(side2_ref[...], q_ref[...], ((1,), (1,)))
    top0 = st0_ref[0:1, :]
    top = jnp.maximum(jnp.max(s_ref[...], axis=0, keepdims=True), jnp.max(ss_ref[...], axis=0, keepdims=True))
    top = jnp.maximum(top, top0)
    st_ref[0:1, :] = top
    w_ref[:n, :] = jnp.exp2((s_ref[...] - top) * k).astype(BF16)
    w_ref[n:, :] = jnp.exp2((ss_ref[...] - top) * k).astype(BF16)
    mix, chosen = products((side2_ref, side_ref), (base_ref[3], base_ref[2]), w_ref, pos_ref, rows)
    m_ref[...] = mix
    for copy in copies:
        copy.wait()
    mix, more = products((a_ref, b_ref), (base_ref[0], base_ref[1]), wo_ref, pos_ref, rows)
    m_ref[...] += mix * jnp.exp2((top0 - top) * k)
    c_ref[...] = (chosen + more).astype(BF16)


def scale_kernel(scale, every_ref, st_ref, m_ref, c_ref, out_ref, loss_ref):
    count = m_ref.shape[1]
    lse = every_ref[:, 0, :count]
    most = jnp.max(lse, axis=0, keepdims=True)
    whole = most + jnp.log(jnp.sum(jnp.exp(lse - most), axis=0, keepdims=True))
    ps = jnp.sum(every_ref[:, 0, count:], axis=0, keepdims=True)
    g = jnp.exp(st_ref[0:1, :] * scale - whole)
    out = (m_ref[...] * g - c_ref[...].astype(F32)).astype(BF16)
    nx, width, _ = out_ref.shape
    piece = width // 4
    for i in range(nx):
        for j in range(4):
            at = (j * nx + i) * piece
            out_ref[i, j * piece : (j + 1) * piece, :] = out[at : at + piece]
    loss_ref[...] = whole - ps


def copy_kernel(x_hbm, out_hbm, x_ref, sems):
    n = out_hbm.shape[0]
    first = pltpu.make_async_copy(x_hbm, x_ref, sems.at[n])
    first.start()
    first.wait()
    copies = [pltpu.make_async_copy(x_ref, out_hbm.at[i], sems.at[i]) for i in range(n)]
    for copy in copies:
        copy.start()
    for copy in copies:
        copy.wait()


def sum_kernel(scale, got_ref, out_ref):
    total = got_ref[0].astype(F32)
    for i in range(1, got_ref.shape[0]):
        total += got_ref[i].astype(F32)
    out_ref[...] = (scale * total).astype(BF16)


def call(body, out, operands, scratch=(), flops=0, vmem=12, hbm_in=(), hbm_out=()):
    def spec(i, o):
        if i in hbm_in:
            return HBM
        return SMEM if o.dtype == jnp.int32 and o.ndim == 1 else VMEM

    kernel = pl.pallas_call(
        body,
        in_specs=[spec(i, o) for i, o in enumerate(operands)],
        out_specs=[HBM if i in hbm_out else VMEM for i in range(len(out))],
        out_shape=[pltpu.HBM(s, d) if i in hbm_out else jax.ShapeDtypeStruct(s, d) for i, (s, d) in enumerate(out)],
        scratch_shapes=[s if not isinstance(s, tuple) else pltpu.VMEM(*s) for s in scratch],
        cost_estimate=pl.CostEstimate(flops=flops, bytes_accessed=4 << 20, transcendentals=0),
        compiler_params=pltpu.CompilerParams(vmem_limit_bytes=vmem << 20),
    )
    operands = [pltpu.with_memory_space_constraint(o, pltpu.HBM) if i in hbm_in else o for i, o in enumerate(operands)]
    return kernel(*operands)


def shards(queries, passages, positive):
    count, width = queries.shape
    rows = passages.shape[0]
    scale = 3.0 / math.sqrt(width)
    nz, nx = lax.axis_size("z"), lax.axis_size("x")
    ny = lax.axis_size("yh") * 2
    x, c = lax.axis_index("x"), lax.axis_index("c")
    y = lax.axis_index("yh") * 2 + lax.axis_index("yl")
    n = nz * rows
    flops = 2 * n * width * count

    def base_of(yy, cc):
        yy = (yy + ny) & (ny - 1)
        return ((((yy >> 1) * nx + x) * nz * 2 + (yy & 1)) * 2 + cc) * rows

    base = jnp.stack(
        [base_of(y, c), base_of(y, 1 - c), base_of(y - 1 + 2 * c, c), base_of(y + 1 - 2 * c, 1 - c), y & 1]
    )
    pos = positive.reshape(1, count)

    theirs = to_sides(queries, ny)
    pos_theirs = to_sides(pos, ny)
    (copies,) = call(
        copy_kernel,
        [((nz, rows, width), BF16)],
        (passages,),
        [((rows, width), BF16), pltpu.SemaphoreType.DMA((nz + 1,))],
        hbm_in=(0,),
        hbm_out=(0,),
    )
    column = lax.all_to_all(copies, "z", split_axis=0, concat_axis=0, tiled=True)
    column, theirs, pos_theirs = lax.optimization_barrier((column, theirs, pos_theirs))
    column = column.reshape(n, width)
    side = to_sides(column, ny)
    column2 = swapped(column)
    members = ny * nx
    st1, weights, stats = call(
        functools.partial(stat_kernel, scale, rows),
        [((8, count), F32), ((2 * n, count), BF16), ((members, 1, 2 * count), F32)],
        (base, column, column2, queries, pos, theirs, pos_theirs),
        [
            ((2 * n, count), F32),
            ((2 * n, count), BF16),
            ((2, 1, 2 * count), F32),
            pltpu.SemaphoreType.DMA((members + 1,)),
        ],
        4 * flops,
        hbm_out=(1, 2),
    )
    every = lax.all_to_all(stats, ("yl", *OUTER), split_axis=0, concat_axis=0, tiled=True)
    side2 = swapped(side)
    queries, side, scores = call(
        side_kernel,
        [(queries.shape, BF16), ((n, width), BF16), ((n, count), F32)],
        (queries, side),
        [pltpu.SemaphoreType.DMA((2,))],
        flops,
        vmem=8,
        hbm_in=(0, 1),
    )
    st, m, ch = call(
        functools.partial(mix_kernel, scale, rows),
        [((8, count), F32), ((width, count), F32), ((width, count), BF16)],
        (base, column, column2, weights, side, scores, side2, queries, pos, st1),
        [
            ((n, count), F32),
            ((2 * n, count), BF16),
            ((n, width), BF16),
            ((n, width), BF16),
            ((2 * n, count), BF16),
            pltpu.SemaphoreType.DMA((3,)),
        ],
        10 * flops,
        vmem=24,
        hbm_in=(1, 2, 3),
    )
    out, loss = call(
        functools.partial(scale_kernel, scale),
        [((nx, width // nx, count), BF16), ((1, count), F32)],
        (every, st, m, ch),
    )
    got = lax.all_to_all(out, "x", split_axis=0, concat_axis=0, tiled=True)
    (out,) = call(functools.partial(sum_kernel, 1.0), [((width // nx, count), BF16)], (got,))
    nyh = ny // 2
    piece = width // nx // nyh
    out = out.reshape(nyh, piece, count)
    got = lax.all_to_all(out, "yh", split_axis=0, concat_axis=0, tiled=True)
    (grad,) = call(functools.partial(sum_kernel, scale), [((piece, count), BF16)], (got,))
    return grad.T, loss.reshape(count)


def solution(mesh):
    devices = mesh.devices
    torus = Mesh(devices.reshape(4, 4, 8, 2, 2), ("yh", "x", "z", "yl", "c"))
    in_specs = (P(INNER, None), P((*OUTER, *INNER), None), P(INNER))
    out_specs = (P(INNER, OUTER), P(INNER))
    return jax.shard_map(shards, mesh=torus, in_specs=in_specs, out_specs=out_specs, check_vma=False)
```

```python
import functools
import math

import jax
import jax.numpy as jnp
from jax import lax
from jax.experimental import pallas as pl
from jax.experimental.pallas import tpu as pltpu
from jax.sharding import Mesh
from jax.sharding import PartitionSpec as P


INNER = ("z", "yl", "c")
OUTER = ("yh", "x")
LANE = ("yh", "yl", "c")
F32, BF16 = jnp.float32, jnp.bfloat16
LOG2E = math.log2(math.e)
VMEM = pl.BlockSpec(memory_space=pltpu.VMEM)
SMEM = pl.BlockSpec(memory_space=pltpu.SMEM)
HBM = pl.BlockSpec(memory_space=pltpu.HBM)


def swapped(x):
    return lax.ppermute(x, "c", [(0, 1), (1, 0)])


def to_sides(x, ny):
    perm = []
    for y in range(ny):
        perm.append((2 * y, 2 * ((y + 1) % ny)))
        perm.append((2 * y + 1, 2 * ((y - 1) % ny) + 1))
    return lax.ppermute(x, LANE, perm)


def dot(a, b, dims):
    return lax.dot_general(a, b, (dims, ((), ())), preferred_element_type=F32)


def hits_of(pos_ref, base, count, rows):
    j = lax.broadcasted_iota(jnp.int32, (count, 1), 0)
    return (j // rows) * (4 * rows) + j % rows == pos_ref[...] - base


def statistics(p_refs, bases, q_ref, pos_ref, s_ref, rows):
    q = q_ref[...]
    top = ps = None
    for i, p_ref in enumerate(p_refs):
        n = p_ref.shape[0]
        s = dot(p_ref[...], q, ((1,), (1,)))
        s_ref[i * n : (i + 1) * n, :] = s
        hit = hits_of(pos_ref, bases[i], n, rows)
        t = jnp.max(s, axis=0, keepdims=True)
        u = jnp.sum(jnp.where(hit, s, 0.0), axis=0, keepdims=True)
        top = t if top is None else jnp.maximum(top, t)
        ps = u if ps is None else ps + u
    return top, ps


def products(p_refs, bases, w_ref, pos_ref, rows):
    mix = chosen = 0.0
    for i, p_ref in enumerate(p_refs):
        n = p_ref.shape[0]
        p = p_ref[...]
        hit = hits_of(pos_ref, bases[i], n, rows).astype(F32).astype(BF16)
        mix += dot(p, w_ref[i * n : (i + 1) * n, :], ((0,), (0,)))
        chosen += dot(p, hit, ((0,), (0,)))
    return mix, chosen


def stat_kernel(scale, rows, base_ref, a_ref, b_ref, q_ref, pos_ref, qf_ref, posf_ref, st_ref, w_hbm, out_ref, s_ref, w_ref, sem):
    bases = (base_ref[0], base_ref[1])
    pieces = []
    for qq, pp in ((q_ref, pos_ref), (qf_ref, posf_ref)):
        top, ps = statistics((a_ref, b_ref), bases, qq, pp, s_ref, rows)
        e = jnp.exp2((s_ref[...] - top) * (scale * LOG2E))
        total = jnp.sum(e, axis=0, keepdims=True)
        if not pieces:
            w_ref[...] = e.astype(BF16)
            copy = pltpu.make_async_copy(w_ref, w_hbm, sem)
            copy.start()
            st_ref[0:1, :] = top
        pieces.append(jnp.concatenate([top * scale + jnp.log(total), ps * scale], axis=1))
    own, theirs = pieces
    lower = base_ref[4] == 0
    half = out_ref.shape[0] // 2
    shape = (half, *own.shape)
    out_ref[:half] = jnp.broadcast_to(jnp.where(lower, own, theirs)[None], shape)
    out_ref[half:] = jnp.broadcast_to(jnp.where(lower, theirs, own)[None], shape)
    copy.wait()


def side_kernel(q_hbm, side_hbm, q_ref, side_ref, s_ref, sems):
    pairs = ((q_hbm, q_ref), (side_hbm, side_ref))
    copies = [pltpu.make_async_copy(src, dst, sems.at[i]) for i, (src, dst) in enumerate(pairs)]
    for copy in copies:
        copy.start()
    for copy in copies:
        copy.wait()
    s_ref[...] = dot(side_ref[...], q_ref[...], ((1,), (1,)))


def mix_kernel(scale, rows, base_ref, a_hbm, b_hbm, wo_hbm, side_ref, ss_ref, side2_ref, q_ref, pos_ref, st0_ref, st_ref, m_ref, c_ref, s_ref, w_ref, a_ref, b_ref, wo_ref, sems):
    pairs = ((a_hbm, a_ref), (b_hbm, b_ref), (wo_hbm, wo_ref))
    copies = [pltpu.make_async_copy(src, dst, sems.at[i]) for i, (src, dst) in enumerate(pairs)]
    for copy in copies:
        copy.start()
    n = side2_ref.shape[0]
    k = scale * LOG2E
    s_ref[...] = dot(side2_ref[...], q_ref[...], ((1,), (1,)))
    top0 = st0_ref[0:1, :]
    top = jnp.maximum(jnp.max(s_ref[...], axis=0, keepdims=True), jnp.max(ss_ref[...], axis=0, keepdims=True))
    top = jnp.maximum(top, top0)
    st_ref[0:1, :] = top
    w_ref[:n, :] = jnp.exp2((s_ref[...] - top) * k).astype(BF16)
    w_ref[n:, :] = jnp.exp2((ss_ref[...] - top) * k).astype(BF16)
    mix, chosen = products((side2_ref, side_ref), (base_ref[3], base_ref[2]), w_ref, pos_ref, rows)
    m_ref[...] = mix
    for copy in copies:
        copy.wait()
    mix, more = products((a_ref, b_ref), (base_ref[0], base_ref[1]), wo_ref, pos_ref, rows)
    m_ref[...] += mix * jnp.exp2((top0 - top) * k)
    c_ref[...] = (chosen + more).astype(BF16)


def scale_kernel(scale, every_ref, st_ref, m_ref, c_ref, out_ref, loss_ref):
    count = m_ref.shape[1]
    lse = every_ref[:, 0, :count]
    most = jnp.max(lse, axis=0, keepdims=True)
    whole = most + jnp.log(jnp.sum(jnp.exp(lse - most), axis=0, keepdims=True))
    ps = jnp.sum(every_ref[:, 0, count:], axis=0, keepdims=True)
    g = jnp.exp(st_ref[0:1, :] * scale - whole)
    out_ref[...] = (m_ref[...] * g - c_ref[...].astype(F32)).astype(BF16)
    loss_ref[...] = whole - ps


def copy_kernel(x_hbm, out_hbm, x_ref, sems):
    n = out_hbm.shape[0]
    first = pltpu.make_async_copy(x_hbm, x_ref, sems.at[n])
    first.start()
    first.wait()
    copies = [pltpu.make_async_copy(x_ref, out_hbm.at[i], sems.at[i]) for i in range(n)]
    for copy in copies:
        copy.start()
    for copy in copies:
        copy.wait()


def sum_kernel(scale, got_ref, out_ref):
    total = got_ref[0].astype(F32)
    for i in range(1, got_ref.shape[0]):
        total += got_ref[i].astype(F32)
    out_ref[...] = (scale * total).astype(BF16)


def call(body, out, operands, scratch=(), flops=0, vmem=12, hbm_in=(), hbm_out=()):
    def spec(i, o):
        if i in hbm_in:
            return HBM
        return SMEM if o.dtype == jnp.int32 and o.ndim == 1 else VMEM

    kernel = pl.pallas_call(
        body,
        in_specs=[spec(i, o) for i, o in enumerate(operands)],
        out_specs=[HBM if i in hbm_out else VMEM for i in range(len(out))],
        out_shape=[pltpu.HBM(s, d) if i in hbm_out else jax.ShapeDtypeStruct(s, d) for i, (s, d) in enumerate(out)],
        scratch_shapes=[s if not isinstance(s, tuple) else pltpu.VMEM(*s) for s in scratch],
        cost_estimate=pl.CostEstimate(flops=flops, bytes_accessed=4 << 20, transcendentals=0),
        compiler_params=pltpu.CompilerParams(vmem_limit_bytes=vmem << 20),
    )
    operands = [pltpu.with_memory_space_constraint(o, pltpu.HBM) if i in hbm_in else o for i, o in enumerate(operands)]
    return kernel(*operands)


def shards(queries, passages, positive):
    count, width = queries.shape
    rows = passages.shape[0]
    scale = 3.0 / math.sqrt(width)
    nz, nx = lax.axis_size("z"), lax.axis_size("x")
    ny = lax.axis_size("yh") * 2
    x, c = lax.axis_index("x"), lax.axis_index("c")
    y = lax.axis_index("yh") * 2 + lax.axis_index("yl")
    n = nz * rows
    flops = 2 * n * width * count

    def base_of(yy, cc):
        yy = (yy + ny) & (ny - 1)
        return ((((yy >> 1) * nx + x) * nz * 2 + (yy & 1)) * 2 + cc) * rows

    base = jnp.stack(
        [base_of(y, c), base_of(y, 1 - c), base_of(y - 1 + 2 * c, c), base_of(y + 1 - 2 * c, 1 - c), y & 1]
    )
    pos = positive.reshape(1, count)

    theirs = to_sides(queries, ny)
    pos_theirs = to_sides(pos, ny)
    (copies,) = call(
        copy_kernel,
        [((nz, rows, width), BF16)],
        (passages,),
        [((rows, width), BF16), pltpu.SemaphoreType.DMA((nz + 1,))],
        hbm_in=(0,),
        hbm_out=(0,),
    )
    column = lax.all_to_all(copies, "z", split_axis=0, concat_axis=0, tiled=True)
    column, theirs, pos_theirs = lax.optimization_barrier((column, theirs, pos_theirs))
    column = column.reshape(n, width)
    side = to_sides(column, ny)
    column2 = swapped(column)
    members = ny * nx
    st1, weights, stats = call(
        functools.partial(stat_kernel, scale, rows),
        [((8, count), F32), ((2 * n, count), BF16), ((members, 1, 2 * count), F32)],
        (base, column, column2, queries, pos, theirs, pos_theirs),
        [((2 * n, count), F32), ((2 * n, count), BF16), pltpu.SemaphoreType.DMA],
        4 * flops,
        hbm_out=(1,),
    )
    every = lax.all_to_all(stats, ("yl", *OUTER), split_axis=0, concat_axis=0, tiled=True)
    side2 = swapped(side)
    queries, side, scores = call(
        side_kernel,
        [(queries.shape, BF16), ((n, width), BF16), ((n, count), F32)],
        (queries, side),
        [pltpu.SemaphoreType.DMA((2,))],
        flops,
        vmem=8,
        hbm_in=(0, 1),
    )
    st, m, ch = call(
        functools.partial(mix_kernel, scale, rows),
        [((8, count), F32), ((width, count), F32), ((width, count), BF16)],
        (base, column, column2, weights, side, scores, side2, queries, pos, st1),
        [
            ((n, count), F32),
            ((2 * n, count), BF16),
            ((n, width), BF16),
            ((n, width), BF16),
            ((2 * n, count), BF16),
            pltpu.SemaphoreType.DMA((3,)),
        ],
        10 * flops,
        vmem=24,
        hbm_in=(1, 2, 3),
    )
    out, loss = call(
        functools.partial(scale_kernel, scale), [((width, count), BF16), ((1, count), F32)], (every, st, m, ch)
    )
    n_outer = members // 2
    out = out.reshape(n_outer, width // n_outer, count)
    got = lax.all_to_all(out, OUTER, split_axis=0, concat_axis=0, tiled=True)
    (grad,) = call(functools.partial(sum_kernel, scale), [((width // n_outer, count), BF16)], (got,))
    return grad.T, loss.reshape(count)


def solution(mesh):
    devices = mesh.devices
    torus = Mesh(devices.reshape(4, 4, 8, 2, 2), ("yh", "x", "z", "yl", "c"))
    in_specs = (P(INNER, None), P((*OUTER, *INNER), None), P(INNER))
    out_specs = (P(INNER, OUTER), P(INNER))
    return jax.shard_map(shards, mesh=torus, in_specs=in_specs, out_specs=out_specs, check_vma=False)
```

```python
import functools
import math

import jax
import jax.numpy as jnp
from jax import lax
from jax.experimental import pallas as pl
from jax.experimental.pallas import tpu as pltpu
from jax.sharding import Mesh
from jax.sharding import PartitionSpec as P


INNER = ("z", "yl", "c")
OUTER = ("yh", "x")
LANE = ("yh", "yl", "c")
F32, BF16 = jnp.float32, jnp.bfloat16
LOG2E = math.log2(math.e)
VMEM = pl.BlockSpec(memory_space=pltpu.VMEM)
SMEM = pl.BlockSpec(memory_space=pltpu.SMEM)
HBM = pl.BlockSpec(memory_space=pltpu.HBM)


def swapped(x):
    return lax.ppermute(x, "c", [(0, 1), (1, 0)])


def to_sides(x, ny):
    perm = []
    for y in range(ny):
        perm.append((2 * y, 2 * ((y + 1) % ny)))
        perm.append((2 * y + 1, 2 * ((y - 1) % ny) + 1))
    return lax.ppermute(x, LANE, perm)


def dot(a, b, dims):
    return lax.dot_general(a, b, (dims, ((), ())), preferred_element_type=F32)


def hits_of(pos_ref, base, count, rows):
    j = lax.broadcasted_iota(jnp.int32, (count, 1), 0)
    return (j // rows) * (4 * rows) + j % rows == pos_ref[...] - base


def statistics(p_refs, bases, q_ref, pos_ref, s_ref, rows):
    q = q_ref[...]
    top = ps = None
    for i, p_ref in enumerate(p_refs):
        n = p_ref.shape[0]
        s = dot(p_ref[...], q, ((1,), (1,)))
        s_ref[i * n : (i + 1) * n, :] = s
        hit = hits_of(pos_ref, bases[i], n, rows)
        t = jnp.max(s, axis=0, keepdims=True)
        u = jnp.sum(jnp.where(hit, s, 0.0), axis=0, keepdims=True)
        top = t if top is None else jnp.maximum(top, t)
        ps = u if ps is None else ps + u
    return top, ps


def products(p_refs, bases, w_ref, pos_ref, rows):
    mix = chosen = 0.0
    for i, p_ref in enumerate(p_refs):
        n = p_ref.shape[0]
        p = p_ref[...]
        hit = hits_of(pos_ref, bases[i], n, rows).astype(F32).astype(BF16)
        mix += dot(p, w_ref[i * n : (i + 1) * n, :], ((0,), (0,)))
        chosen += dot(p, hit, ((0,), (0,)))
    return mix, chosen


def stat_kernel(scale, rows, base_ref, a_ref, b_ref, q_ref, pos_ref, qf_ref, posf_ref, st_ref, w_hbm, out_ref, s_ref, w_ref, sem):
    bases = (base_ref[0], base_ref[1])
    pieces = []
    for qq, pp in ((q_ref, pos_ref), (qf_ref, posf_ref)):
        top, ps = statistics((a_ref, b_ref), bases, qq, pp, s_ref, rows)
        e = jnp.exp2((s_ref[...] - top) * (scale * LOG2E))
        total = jnp.sum(e, axis=0, keepdims=True)
        if not pieces:
            w_ref[...] = e.astype(BF16)
            copy = pltpu.make_async_copy(w_ref, w_hbm, sem)
            copy.start()
            st_ref[0:1, :] = top
        pieces.append(jnp.concatenate([top * scale + jnp.log(total), ps * scale], axis=1))
    own, theirs = pieces
    lower = base_ref[4] == 0
    half = out_ref.shape[0] // 2
    shape = (half, *own.shape)
    out_ref[:half] = jnp.broadcast_to(jnp.where(lower, own, theirs)[None], shape)
    out_ref[half:] = jnp.broadcast_to(jnp.where(lower, theirs, own)[None], shape)
    copy.wait()


def side_kernel(q_hbm, side_hbm, q_ref, side_ref, s_ref, sems):
    pairs = ((q_hbm, q_ref), (side_hbm, side_ref))
    copies = [pltpu.make_async_copy(src, dst, sems.at[i]) for i, (src, dst) in enumerate(pairs)]
    for copy in copies:
        copy.start()
    for copy in copies:
        copy.wait()
    s_ref[...] = dot(side_ref[...], q_ref[...], ((1,), (1,)))


def mix_kernel(scale, rows, base_ref, a_hbm, b_hbm, wo_hbm, side_ref, ss_ref, side2_ref, q_ref, pos_ref, st0_ref, st_ref, m_ref, c_ref, s_ref, w_ref, a_ref, b_ref, wo_ref, sems):
    pairs = ((a_hbm, a_ref), (b_hbm, b_ref), (wo_hbm, wo_ref))
    copies = [pltpu.make_async_copy(src, dst, sems.at[i]) for i, (src, dst) in enumerate(pairs)]
    for copy in copies:
        copy.start()
    n = side2_ref.shape[0]
    k = scale * LOG2E
    s_ref[...] = dot(side2_ref[...], q_ref[...], ((1,), (1,)))
    top0 = st0_ref[0:1, :]
    top = jnp.maximum(jnp.max(s_ref[...], axis=0, keepdims=True), jnp.max(ss_ref[...], axis=0, keepdims=True))
    top = jnp.maximum(top, top0)
    st_ref[0:1, :] = top
    w_ref[:n, :] = jnp.exp2((s_ref[...] - top) * k).astype(BF16)
    w_ref[n:, :] = jnp.exp2((ss_ref[...] - top) * k).astype(BF16)
    mix, chosen = products((side2_ref, side_ref), (base_ref[3], base_ref[2]), w_ref, pos_ref, rows)
    m_ref[...] = mix
    for copy in copies:
        copy.wait()
    mix, more = products((a_ref, b_ref), (base_ref[0], base_ref[1]), wo_ref, pos_ref, rows)
    m_ref[...] += mix * jnp.exp2((top0 - top) * k)
    c_ref[...] = (chosen + more).astype(BF16)


def scale_kernel(scale, every_ref, st_ref, m_ref, c_ref, out_ref, loss_ref):
    count = m_ref.shape[1]
    lse = every_ref[:, 0, :count]
    most = jnp.max(lse, axis=0, keepdims=True)
    whole = most + jnp.log(jnp.sum(jnp.exp(lse - most), axis=0, keepdims=True))
    ps = jnp.sum(every_ref[:, 0, count:], axis=0, keepdims=True)
    g = jnp.exp(st_ref[0:1, :] * scale - whole)
    out = (m_ref[...] * g - c_ref[...].astype(F32)).astype(BF16)
    nx, width, _ = out_ref.shape
    piece = width // 4
    for i in range(nx):
        for j in range(4):
            at = (j * nx + i) * piece
            out_ref[i, j * piece : (j + 1) * piece, :] = out[at : at + piece]
    loss_ref[...] = whole - ps


def copy_kernel(x_ref, out_hbm, sems):
    n = out_hbm.shape[0]
    copies = [pltpu.make_async_copy(x_ref, out_hbm.at[i], sems.at[i]) for i in range(n)]
    for copy in copies:
        copy.start()
    for copy in copies:
        copy.wait()


def sum_kernel(scale, got_ref, out_ref):
    total = got_ref[0].astype(F32)
    for i in range(1, got_ref.shape[0]):
        total += got_ref[i].astype(F32)
    out_ref[...] = (scale * total).astype(BF16)


def call(body, out, operands, scratch=(), flops=0, vmem=12, hbm_in=(), hbm_out=()):
    def spec(i, o):
        if i in hbm_in:
            return HBM
        return SMEM if o.dtype == jnp.int32 and o.ndim == 1 else VMEM

    kernel = pl.pallas_call(
        body,
        in_specs=[spec(i, o) for i, o in enumerate(operands)],
        out_specs=[HBM if i in hbm_out else VMEM for i in range(len(out))],
        out_shape=[pltpu.HBM(s, d) if i in hbm_out else jax.ShapeDtypeStruct(s, d) for i, (s, d) in enumerate(out)],
        scratch_shapes=[s if not isinstance(s, tuple) else pltpu.VMEM(*s) for s in scratch],
        cost_estimate=pl.CostEstimate(flops=flops, bytes_accessed=4 << 20, transcendentals=0),
        compiler_params=pltpu.CompilerParams(vmem_limit_bytes=vmem << 20),
    )
    operands = [pltpu.with_memory_space_constraint(o, pltpu.HBM) if i in hbm_in else o for i, o in enumerate(operands)]
    return kernel(*operands)


def shards(queries, passages, positive):
    count, width = queries.shape
    rows = passages.shape[0]
    scale = 3.0 / math.sqrt(width)
    nz, nx = lax.axis_size("z"), lax.axis_size("x")
    ny = lax.axis_size("yh") * 2
    x, c = lax.axis_index("x"), lax.axis_index("c")
    y = lax.axis_index("yh") * 2 + lax.axis_index("yl")
    n = nz * rows
    flops = 2 * n * width * count

    def base_of(yy, cc):
        yy = (yy + ny) & (ny - 1)
        return ((((yy >> 1) * nx + x) * nz * 2 + (yy & 1)) * 2 + cc) * rows

    base = jnp.stack(
        [base_of(y, c), base_of(y, 1 - c), base_of(y - 1 + 2 * c, c), base_of(y + 1 - 2 * c, 1 - c), y & 1]
    )
    pos = positive.reshape(1, count)

    theirs = to_sides(queries, ny)
    pos_theirs = to_sides(pos, ny)
    (copies,) = call(
        copy_kernel, [((nz, rows, width), BF16)], (passages,), [pltpu.SemaphoreType.DMA((nz,))], hbm_out=(0,)
    )
    column = lax.all_to_all(copies, "z", split_axis=0, concat_axis=0, tiled=True)
    column, theirs, pos_theirs = lax.optimization_barrier((column, theirs, pos_theirs))
    column = column.reshape(n, width)
    side = to_sides(column, ny)
    column2 = swapped(column)
    members = ny * nx
    st1, weights, stats = call(
        functools.partial(stat_kernel, scale, rows),
        [((8, count), F32), ((2 * n, count), BF16), ((members, 1, 2 * count), F32)],
        (base, column, column2, queries, pos, theirs, pos_theirs),
        [((2 * n, count), F32), ((2 * n, count), BF16), pltpu.SemaphoreType.DMA],
        4 * flops,
        hbm_out=(1,),
    )
    every = lax.all_to_all(stats, ("yl", *OUTER), split_axis=0, concat_axis=0, tiled=True)
    side2 = swapped(side)
    queries, side, scores = call(
        side_kernel,
        [(queries.shape, BF16), ((n, width), BF16), ((n, count), F32)],
        (queries, side),
        [pltpu.SemaphoreType.DMA((2,))],
        flops,
        vmem=8,
        hbm_in=(0, 1),
    )
    st, m, ch = call(
        functools.partial(mix_kernel, scale, rows),
        [((8, count), F32), ((width, count), F32), ((width, count), BF16)],
        (base, column, column2, weights, side, scores, side2, queries, pos, st1),
        [
            ((n, count), F32),
            ((2 * n, count), BF16),
            ((n, width), BF16),
            ((n, width), BF16),
            ((2 * n, count), BF16),
            pltpu.SemaphoreType.DMA((3,)),
        ],
        10 * flops,
        vmem=24,
        hbm_in=(1, 2, 3),
    )
    out, loss = call(
        functools.partial(scale_kernel, scale),
        [((nx, width // nx, count), BF16), ((1, count), F32)],
        (every, st, m, ch),
    )
    got = lax.all_to_all(out, "x", split_axis=0, concat_axis=0, tiled=True)
    (out,) = call(functools.partial(sum_kernel, 1.0), [((width // nx, count), BF16)], (got,))
    nyh = ny // 2
    piece = width // nx // nyh
    out = out.reshape(nyh, piece, count)
    got = lax.all_to_all(out, "yh", split_axis=0, concat_axis=0, tiled=True)
    (grad,) = call(functools.partial(sum_kernel, scale), [((piece, count), BF16)], (got,))
    return grad.T, loss.reshape(count)


def solution(mesh):
    devices = mesh.devices
    torus = Mesh(devices.reshape(4, 4, 8, 2, 2), ("yh", "x", "z", "yl", "c"))
    in_specs = (P(INNER, None), P((*OUTER, *INNER), None), P(INNER))
    out_specs = (P(INNER, OUTER), P(INNER))
    return jax.shard_map(shards, mesh=torus, in_specs=in_specs, out_specs=out_specs, check_vma=False)
```
